32 devices in a mesh: parts: 2 (over y), row: 4 (over z), col: 2 (over x), rhs: 2 (over core).
Axes of the slice: x: 2, y: 2, z: 4, core: 2. Of those that a mesh axis runs over, the one named last changes fastest.
Arguments:
- blocks: bfloat16 [8, 2, 96, 128, 128], P(('parts', 'row'), 'col'), parts along dimension 0, as said below
- block_rows: int32 [8, 2, 96], P(('parts', 'row'), 'col'), parts along dimension 0, may hold values from 0 to 127, as said below
- block_cols: int32 [8, 2, 96], P(('parts', 'row'), 'col'), parts along dimension 0, may hold values from 0 to 255, as said below
- counts: int32 [8, 2], P(('parts', 'row'), 'col'), parts along dimension 0, may hold values from 1 to 96, as said below
- diagonal: float32 [131072], P(('parts', 'row', 'col')), parts along dimension 0, may hold values from 1.2 to 4
- target: float32 [131072, 256], P(('parts', 'row', 'col'), 'rhs'), parts along dimension 0, may hold values from -6 to 6
Outputs:
- solution: float32 [131072, 256], P(('parts', 'row', 'col'), 'rhs'), parts along dimension 0
- residual: float32 [131072, 256], P(('parts', 'row', 'col'), 'rhs'), parts along dimension 0
The draws below stay inside these ranges and needn't reach their ends.
There are 2 independent parts, one for each index of `parts`. The reference program is written for one: setup_inputs(seed, part) draws one part's arguments, and reference() takes and returns one part's arrays. A program takes and returns all parts, laid end to end along the dimension named above; each array names one. Nothing has to cross between parts.
Inputs may be any that keep to these rules, and one draw needn't show every extreme that they name: Each tile's used slots are its first counts slots; the busiest tile has exactly 96. `block_rows`: used slots of one tile name distinct blocks on or above the diagonal. `block_cols`: see block_rows. `blocks`: unused slots hold values that do not enter the operator; the operator is positive definite.
All inputs are finite; a program needn't handle non-finite values.
Results may differ from the reference program's by a relative error of at most 0.0045.
Values may be sent and summed in bfloat16 or wider, within the bound.
A program may use at most 128 MiB of HBM per device.

```python
import math
import jax
import jax.numpy as jnp
from jax import lax

LAT = 65536
BS = 128
RHS = 256
BLK_DEV = 96
ITERS = 2
RB = 128
CB = 256
QB = 64
N_ROW = 4
N_COL = 2


def pattern(key):
    grid_rows = CB // QB
    grid_cols = RB // QB
    pairs = RB * CB
    inner = jnp.arange(pairs, dtype=jnp.int32)
    local_row = inner // CB
    local_col = inner % CB
    ridx = jnp.arange(grid_rows, dtype=jnp.int32)[:, None, None]
    cidx = jnp.arange(grid_cols, dtype=jnp.int32)[None, :, None]
    upper_i = ridx * RB + local_row[None, None, :]
    upper_j = (local_col[None, None, :] // QB * grid_cols + cidx) * QB + local_col[None, None, :] % QB
    valid = (upper_i <= upper_j).astype(jnp.int32)
    upper = jnp.sum(valid, axis=2)
    cap = jnp.minimum(BLK_DEV, upper).astype(jnp.int32)
    low = jnp.maximum(1, cap // 2).astype(jnp.int32)
    drawn = jax.random.randint(jax.random.fold_in(key, 5), (grid_rows, grid_cols), low, cap + 1, dtype=jnp.int32)
    flat = jnp.arange(grid_rows * grid_cols, dtype=jnp.int32).reshape(grid_rows, grid_cols)
    busiest = jnp.argmax(upper.reshape(-1)).astype(jnp.int32)
    counts = jnp.where(flat == busiest, BLK_DEV, drawn).astype(jnp.int32)
    span = 2 ** 28 // pairs
    noise = jax.random.randint(jax.random.fold_in(key, 7), (grid_rows, grid_cols, pairs), 0, span, dtype=jnp.int32)
    score = valid * 2 ** 28 + noise * pairs + inner[None, None, :]
    _, picked = lax.top_k(score, BLK_DEV)
    picked = picked.astype(jnp.int32)
    return (picked // CB, picked % CB, counts)


def draw_block_rows(key, part):
    return pattern(key)[0]


def draw_block_cols(key, part):
    return pattern(key)[1]


def draw_counts(key, part):
    return pattern(key)[2]


def draw_blocks(key, part):
    grid_rows = CB // QB
    grid_cols = RB // QB
    amp = 0.6 * (RB * CB / (BLK_DEV * LAT)) ** 0.5
    shape = (grid_rows, grid_cols, BLK_DEV, BS, BS)
    values = jax.random.uniform(jax.random.fold_in(key, 11), shape, jnp.float32, -1.0, 1.0)
    return (values * amp).astype(jnp.bfloat16)


def shard_levels(stream_key, dims, shards, least, largest):
    level = 1.0
    for axis_at, parts in shards:
        steps = jax.random.uniform(jax.random.fold_in(jax.random.fold_in(stream_key, 6), axis_at), (parts,), jnp.float32, least / len(shards), largest / len(shards))
        level = level * jnp.repeat(jnp.exp(steps), dims[axis_at] // parts).reshape((-1,) + (1,) * (len(dims) - 1 - axis_at))
    return level


def gaussian(rng, extent, width, limit, pieces=(), kind=jnp.bfloat16):
    loudness = shard_levels(rng, extent, pieces, -0.22, 0.18) if pieces else 1.0
    entries = jax.random.normal(rng, extent, jnp.float32) * width * loudness
    return jnp.minimum(jnp.maximum(entries, -limit), limit).astype(kind)


def setup_inputs(seed: int = 0, part: int = 0) -> dict:
    streams_of = jax.random.split(jax.random.key(seed), 7)
    own_keys = jax.random.split(jax.random.fold_in(streams_of[6], part), 7)
    return {
        "blocks": draw_blocks(jax.random.fold_in(jax.random.fold_in(streams_of[6], part), 71), part),
        "block_rows": draw_block_rows(jax.random.fold_in(jax.random.fold_in(streams_of[6], part), 71), part),
        "block_cols": draw_block_cols(jax.random.fold_in(jax.random.fold_in(streams_of[6], part), 71), part),
        "counts": draw_counts(jax.random.fold_in(jax.random.fold_in(streams_of[6], part), 71), part),
        "diagonal": jnp.clip(jnp.exp(math.log(4.0) - 1.2039728 * jax.random.uniform(own_keys[4], (LAT,), jnp.float32) ** shard_levels(own_keys[4], (LAT,), ((0, 8),), -0.2, 0.2)), 1.2, 4.0),
        "target": gaussian(own_keys[5], (LAT, RHS), 1.0, 6.0, ((0, 8), (1, 2)), jnp.float32),
    }


def tile_terms(blk, rows, cols, count, prow, pcol, nrb, ncb):
    hi = lax.Precision.HIGHEST
    valid = jnp.arange(blk.shape[0]) < count
    prod = jnp.einsum('kab,kbc->kac', blk, pcol[cols], precision=hi)
    rows_hot = ((rows[None, :] == jnp.arange(nrb)[:, None]) & valid[None, :]).astype(jnp.float32)
    direct = jnp.einsum('ik,kac->iac', rows_hot, prod, precision=hi)
    tprod = jnp.einsum('kba,kbc->kac', blk, prow[rows], precision=hi)
    cols_hot = ((cols[None, :] == jnp.arange(ncb)[:, None]) & valid[None, :]).astype(jnp.float32)
    mirrored = jnp.einsum('jk,kac->jac', cols_hot, tprod, precision=hi)
    return direct, mirrored


def rounded(value):
    return lax.optimization_barrier(value.astype(jnp.bfloat16)).astype(jnp.float32)


def operate(blocks, block_rows, block_cols, counts, diagonal, field):
    ncols = field.shape[1]
    grid = rounded(field).reshape(N_ROW, N_COL, QB * BS, ncols)

    def step(total, tile):
        ridx = tile // N_COL
        cidx = tile % N_COL
        prow = lax.dynamic_index_in_dim(grid, ridx, 0, keepdims=False).reshape(RB, BS, ncols)
        pcol = lax.dynamic_index_in_dim(grid, cidx, 1, keepdims=False).reshape(CB, BS, ncols)
        blk = blocks[ridx, cidx].astype(jnp.float32)
        direct, mirrored = tile_terms(blk, block_rows[ridx, cidx], block_cols[ridx, cidx], counts[ridx, cidx], prow, pcol, RB, CB)
        total = total.at[ridx].add(rounded(direct).reshape(N_COL, QB * BS, ncols))
        total = total.at[:, cidx].add(rounded(mirrored).reshape(N_ROW, QB * BS, ncols))
        return total, None

    start = jnp.zeros((N_ROW, N_COL, QB * BS, ncols), jnp.float32)
    total, _ = lax.scan(step, start, jnp.arange(N_ROW * N_COL, dtype=jnp.int32))
    return diagonal[:, None] * field + total.reshape(LAT, ncols)


def reference(blocks, block_rows, block_cols, counts, diagonal, target):
    solution = jnp.zeros_like(target)
    residual = target
    direction = target
    norm_now = jnp.sum(residual * residual, axis=0)
    for step in range(ITERS):
        image = operate(blocks, block_rows, block_cols, counts, diagonal, direction)
        alpha = norm_now / jnp.sum(direction * image, axis=0)
        solution = solution + alpha * direction
        residual = residual - alpha * image
        if step + 1 < ITERS:
            norm_next = jnp.sum(residual * residual, axis=0)
            direction = residual + (norm_next / norm_now) * direction
            norm_now = norm_next
    return solution, residual
```

```python
import functools
import jax
import jax.numpy as jnp
from jax import lax
from jax.experimental import pallas as pl
from jax.experimental.pallas import tpu as pltpu
from jax.sharding import PartitionSpec as P

ITERS = 2
UNROLL = 8
GATHER_BYTES = 32 * 2**20


def operate_kernel(slots, irow_ref, icol_ref, count_ref, blocks_ref, low_ref, image_ref):
    tile = pl.program_id(0)

    @pl.when(tile == 0)
    def _():
        image_ref[...] = jnp.zeros_like(image_ref)

    count = count_ref[tile]

    def group(step, carry):
        base = step * UNROLL
        terms = []
        for u in range(UNROLL):
            k = base + u
            i = irow_ref[tile * slots + k]
            j = icol_ref[tile * slots + k]
            block = blocks_ref[0, k]
            direct = lax.dot_general(
                low_ref[j], block, (((1,), (1,)), ((), ())), preferred_element_type=jnp.float32
            )
            mirrored = lax.dot_general(
                low_ref[i], block, (((1,), (0,)), ((), ())), preferred_element_type=jnp.float32
            )
            terms.append((k < count, i, j, direct, mirrored))
        for used, i, j, direct, mirrored in terms:
            image_ref[i] += jnp.where(used, direct, 0.0)
            image_ref[j] += jnp.where(used, mirrored, 0.0)
        return carry

    lax.fori_loop(0, (count + UNROLL - 1) // UNROLL, group, 0)


def operate(blocks, irow, icol, count, low):
    tiles, slots, width, _ = blocks.shape
    return pl.pallas_call(
        functools.partial(operate_kernel, slots),
        out_shape=jax.ShapeDtypeStruct(low.shape, jnp.float32),
        grid_spec=pltpu.PrefetchScalarGridSpec(
            num_scalar_prefetch=3,
            grid=(tiles,),
            in_specs=[
                pl.BlockSpec((1, slots, width, width), lambda t, *_: (t, 0, 0, 0)),
                pl.BlockSpec(low.shape, lambda t, *_: (0, 0, 0)),
            ],
            out_specs=pl.BlockSpec(low.shape, lambda t, *_: (0, 0, 0)),
        ),
        compiler_params=pltpu.CompilerParams(vmem_limit_bytes=40 * 2**20),
    )(irow, icol, count, blocks, low)


def by_columns(blocks, block_rows, block_cols, counts, diagonal, target):
    grid = ("row", "col")
    nrow = lax.axis_size("row")
    ncol = lax.axis_size("col")
    nrhs = lax.axis_size("rhs")
    devices = nrow * ncol
    stored = blocks[0, 0]
    slots, width, _ = stored.shape
    quarter = target.shape[0] // width
    own = target.shape[1] // devices
    row_blocks = ncol * quarter

    half = slots // nrhs
    piece = lax.dynamic_slice_in_dim(stored, lax.axis_index("rhs") * half, half, axis=0)
    tiles = lax.all_gather(piece, grid, axis=0, tiled=False)
    tiles = lax.all_gather(tiles, "rhs", axis=0, tiled=False)
    tiles = tiles.reshape(nrhs * devices, half, width, width)

    row, col = lax.axis_index("row"), lax.axis_index("col")
    irow = row * row_blocks + block_rows[0, 0]
    jcol = block_cols[0, 0]
    icol = (jcol // quarter * ncol + col) * quarter + jcol % quarter
    names = jnp.concatenate([irow, icol, counts[0]])
    names = lax.all_gather(names, grid, axis=0, tiled=False)

    def halves(index):
        return index.reshape(devices, nrhs, half).transpose(1, 0, 2).reshape(-1)

    rows_all = halves(names[:, :slots])
    cols_all = halves(names[:, slots : 2 * slots])
    count = names[:, 2 * slots]
    count_all = jnp.clip(
        count[None, :] - jnp.arange(nrhs, dtype=jnp.int32)[:, None] * half, 0, half
    ).reshape(-1)

    diag = lax.all_gather(diagonal, grid, axis=0, tiled=True).reshape(-1, 1, width)

    def outward(field):
        parcel = field.reshape(quarter, width, devices, own).transpose(2, 0, 3, 1)
        return lax.all_to_all(parcel, grid, split_axis=0, concat_axis=0, tiled=True).reshape(
            devices * quarter, own, width
        )

    def inner(a, b):
        return jnp.sum(a * b, axis=(0, 2), keepdims=True)

    residual = outward(target)
    direction = residual
    answer = jnp.zeros_like(residual)
    norm_now = inner(residual, residual)
    for step in range(ITERS):
        product = operate(tiles, rows_all, cols_all, count_all, direction.astype(jnp.bfloat16))
        image = diag * direction + product
        alpha = norm_now / inner(direction, image)
        answer = answer + alpha * direction
        residual = residual - alpha * image
        if step + 1 < ITERS:
            norm_next = inner(residual, residual)
            direction = residual + norm_next / norm_now * direction
            norm_now = norm_next
    both = jnp.stack([answer, residual]).astype(jnp.bfloat16)
    parcel = both.reshape(2, devices, quarter, own, width)
    home = lax.all_to_all(parcel, grid, split_axis=1, concat_axis=1, tiled=True)
    home = home.transpose(0, 2, 4, 1, 3).reshape(2, quarter * width, devices * own)
    home = home.astype(jnp.float32)
    return (home[0], home[1])


def one_hot_slots(indices, valid, extent):
    return ((indices[None, :] == jnp.arange(extent)[:, None]) & valid[None, :]).astype(jnp.float32)


def on_device(blocks, block_rows, block_cols, counts, diagonal, target):
    highest = lax.Precision.HIGHEST
    nrow = lax.axis_size("row")
    ncol = lax.axis_size("col")
    tile_bytes = blocks[0, 0].size * blocks.dtype.itemsize
    if (
        nrow * ncol * tile_bytes <= GATHER_BYTES
        and target.shape[1] % (16 * nrow * ncol) == 0
        and blocks.shape[2] % (UNROLL * lax.axis_size("rhs")) == 0
    ):
        return by_columns(blocks, block_rows, block_cols, counts, diagonal, target)
    stored = blocks[0, 0]
    slots = stored.shape[0]
    width = stored.shape[1]
    local = target.shape[0]
    ncols = target.shape[1]
    quarter = local // width
    row_blocks = ncol * quarter
    col_blocks = nrow * quarter
    valid = jnp.arange(slots) < counts[0, 0]
    rows_hot = one_hot_slots(block_rows[0, 0], valid, row_blocks)
    cols_hot = one_hot_slots(block_cols[0, 0], valid, col_blocks)

    def squares(vector):
        return lax.psum(jnp.sum(vector * vector, axis=0), ("row", "col"))

    solution = jnp.zeros_like(target)
    residual = target
    direction = target
    norm_now = squares(residual)
    for step in range(ITERS):
        operate_field_low = direction.astype(jnp.bfloat16)
        direct_gathered = lax.all_gather(operate_field_low, "row", axis=0, tiled=True).reshape(
            col_blocks, width, ncols
        )
        prod = jnp.einsum(
            "kab,kbc->kac",
            stored,
            direct_gathered[block_cols[0, 0]],
            preferred_element_type=jnp.float32,
        )
        direct_partial_value = jnp.einsum("ik,kac->iac", rows_hot, prod, precision=highest)
        direct = lax.psum_scatter(
            direct_partial_value.reshape(row_blocks * width, ncols).astype(jnp.bfloat16),
            "col",
            scatter_dimension=0,
            tiled=True,
        ).astype(jnp.float32)
        gathered = lax.all_gather(operate_field_low, "col", axis=0, tiled=True).reshape(
            row_blocks, width, ncols
        )
        tprod = jnp.einsum(
            "kba,kbc->kac", stored, gathered[block_rows[0, 0]], preferred_element_type=jnp.float32
        )
        partial_value = jnp.einsum("jk,kac->jac", cols_hot, tprod, precision=highest)
        parcel = partial_value.astype(jnp.bfloat16).reshape(nrow, local, ncols)
        mirrored = jnp.sum(
            lax.all_to_all(parcel, "row", split_axis=0, concat_axis=0, tiled=True).astype(
                jnp.float32
            ),
            axis=0,
        )
        image = diagonal[:, None] * direction + direct + mirrored
        curve = lax.psum(jnp.sum(direction * image, axis=0), ("row", "col"))
        alpha = norm_now / curve
        solution = solution + alpha * direction
        residual = residual - alpha * image
        if step + 1 < ITERS:
            norm_next = squares(residual)
            direction = residual + norm_next / norm_now * direction
            norm_now = norm_next
    return (solution, residual)


def solution(mesh):
    return jax.shard_map(
        on_device,
        mesh=mesh,
        in_specs=(
            P(("parts", "row"), "col", None, None, None),
            P(("parts", "row"), "col", None),
            P(("parts", "row"), "col", None),
            P(("parts", "row"), "col"),
            P(("parts", "row", "col")),
            P(("parts", "row", "col"), "rhs"),
        ),
        out_specs=(P(("parts", "row", "col"), "rhs"), P(("parts", "row", "col"), "rhs")),
        check_vma=False,
    )
```

```python
import functools
import jax
import jax.numpy as jnp
from jax import lax
from jax.experimental import pallas as pl
from jax.experimental.pallas import tpu as pltpu
from jax.sharding import PartitionSpec as P

ITERS = 2
UNROLL = 8
GATHER_BYTES = 32 * 2**20
MESH = pl.DeviceIdType.MESH
ANY = pl.BlockSpec(memory_space=pl.ANY)


def spread_kernel(
    nrow, stored, parcel, names, diag,
    tiles, field, all_names, all_diag,
    ring_send, ring_recv, send, recv, own_sem,
):
    devices = 2 * nrow
    row, col, core = lax.axis_index("row"), lax.axis_index("col"), lax.axis_index("rhs")
    me = row * 2 + col
    place = jnp.where(col == 0, row, devices - 1 - row)

    def device_at(place):
        place = lax.rem(place + devices, devices)
        back = place >= nrow
        return jnp.where(back, devices - 1 - place, place), jnp.where(back, 1, 0)

    def peer(offset):
        other = lax.rem(me + offset, devices)
        return {"row": other // 2, "col": lax.rem(other, 2)}

    barrier = pltpu.get_barrier_semaphore()
    for offset in range(1, devices):
        pl.semaphore_signal(barrier, inc=1, device_id=peer(offset), device_id_type=MESH)
    pl.semaphore_wait(barrier, devices - 1)

    half = tiles.shape[1]
    quart = half // 2
    hops = []

    def hop(way, step):
        r, c = device_at(place + (1 if way == 0 else -1))
        if step == 0:
            source = stored.at[pl.ds(way * quart, quart), core]
            origin = me
        else:
            orow, ocol = device_at(place + (-step if way == 0 else step))
            origin = orow * 2 + ocol
            source = tiles.at[origin, pl.ds(way * quart, quart)]
        copy = pltpu.make_async_remote_copy(
            src_ref=source,
            dst_ref=tiles.at[origin, pl.ds(way * quart, quart)],
            send_sem=ring_send.at[way, step],
            recv_sem=ring_recv.at[way, step],
            device_id={"row": r, "col": c},
            device_id_type=MESH,
        )
        copy.start()
        return copy

    now = [hop(0, 0), hop(1, 0)]
    straight = []
    pairs = ((names, all_names, False), (diag, all_diag, False), (parcel, field, True))
    for n, (source, target, apart) in enumerate(pairs):
        for offset in range(1, devices):
            copy = pltpu.make_async_remote_copy(
                src_ref=source.at[lax.rem(me + offset, devices)] if apart else source,
                dst_ref=target.at[me],
                send_sem=send.at[n, offset - 1],
                recv_sem=recv.at[n, offset - 1],
                device_id=peer(offset),
                device_id_type=MESH,
            )
            copy.start()
            straight.append(copy)
    local = []
    owns = (
        (stored.at[:, core], tiles.at[me]),
        (names, all_names.at[me]),
        (diag, all_diag.at[me]),
        (parcel.at[me], field.at[me]),
    )
    for n, (source, target) in enumerate(owns):
        copy = pltpu.make_async_copy(source, target, own_sem.at[n])
        copy.start()
        local.append(copy)
    for step in range(1, devices):
        for way in range(2):
            now[way].wait_recv()
            if step < devices - 1:
                hops.append(now[way])
                now[way] = hop(way, step)
    hops += now
    for copy in hops:
        copy.wait_send()
    for copy in straight:
        copy.wait()
    for copy in local:
        copy.wait()


def spread(stored, parcel, names, diag):
    nrow = lax.axis_size("row")
    devices = 2 * nrow
    half, cores, width, _ = stored.shape
    return pl.pallas_call(
        functools.partial(spread_kernel, nrow),
        out_shape=(
            jax.ShapeDtypeStruct((devices, half, width, width), stored.dtype),
            jax.ShapeDtypeStruct(parcel.shape, parcel.dtype),
            jax.ShapeDtypeStruct((devices,) + names.shape, names.dtype),
            jax.ShapeDtypeStruct((devices,) + diag.shape, diag.dtype),
        ),
        in_specs=[ANY] * 4,
        out_specs=[ANY] * 4,
        scratch_shapes=[
            pltpu.SemaphoreType.DMA((2, devices - 1)),
            pltpu.SemaphoreType.DMA((2, devices - 1)),
            pltpu.SemaphoreType.DMA((3, devices - 1)),
            pltpu.SemaphoreType.DMA((3, devices - 1)),
            pltpu.SemaphoreType.DMA((4,)),
        ],
        compiler_params=pltpu.CompilerParams(collective_id=0, has_side_effects=True),
    )(stored, parcel, names, diag)


def pack_kernel(target_ref, parcel_ref):
    devices, blocks, own, width = parcel_ref.shape
    for b in range(blocks):
        low = target_ref[b].T.astype(jnp.bfloat16)
        parcel_ref[:, b] = low.reshape(devices, own, width)


def pack(target, devices):
    blocks, width, columns = target.shape
    own = columns // devices
    step = min(8, blocks)
    return pl.pallas_call(
        pack_kernel,
        out_shape=jax.ShapeDtypeStruct((devices, blocks, own, width), jnp.bfloat16),
        grid=(blocks // step,),
        in_specs=[pl.BlockSpec((step, width, columns), lambda g: (g, 0, 0))],
        out_specs=pl.BlockSpec((devices, step, own, width), lambda g: (0, g, 0, 0)),
    )(target)


def finish_kernel(target_ref, diag_ref, first_ref, second_ref, scale_ref, answer_ref, residual_ref):
    blocks, width, columns = target_ref.shape
    alpha1, alpha2, beta = scale_ref[0:1], scale_ref[1:2], scale_ref[2:3]
    for b in range(blocks):
        target = target_ref[b]
        diag = jnp.transpose(jnp.broadcast_to(diag_ref[pl.ds(b, 1), :], (columns, width)))
        first = first_ref[:, b].reshape(columns, width).astype(jnp.float32).T
        second = second_ref[:, b].reshape(columns, width).astype(jnp.float32).T
        lost = target - target.astype(jnp.bfloat16).astype(jnp.float32)
        lost1 = lost - alpha1 * diag * lost
        answer_ref[b] = alpha1 * target + alpha2 * (first + lost1 + beta * target)
        residual_ref[b] = second + lost1 - alpha2 * diag * (lost1 + beta * lost)


def finish(target, diag, first, second, scales):
    blocks, width, columns = target.shape
    devices, _, own, _ = first.shape
    step = min(8, blocks)
    whole = pl.BlockSpec((step, width, columns), lambda g: (g, 0, 0))
    part = pl.BlockSpec((devices, step, own, width), lambda g: (0, g, 0, 0))
    return pl.pallas_call(
        finish_kernel,
        out_shape=(jax.ShapeDtypeStruct(target.shape, jnp.float32),) * 2,
        grid=(blocks // step,),
        in_specs=[
            whole,
            pl.BlockSpec((step, width), lambda g: (g, 0)),
            part,
            part,
            pl.BlockSpec(scales.shape, lambda g: (0, 0)),
        ],
        out_specs=(whole, whole),
    )(target, diag, first, second, scales)


def operate_kernel(slots, irow_ref, icol_ref, count_ref, blocks_ref, mine_ref, theirs_ref,
                   image_ref, away_ref, sum_ref):
    tile = pl.program_id(0)
    own = mine_ref.shape[1]

    @pl.when(tile == 0)
    def _():
        image_ref[...] = jnp.zeros_like(image_ref)
        sum_ref[...] = jnp.zeros_like(sum_ref)

    count = count_ref[tile]

    def group(step, carry):
        base = step * UNROLL
        terms = []
        for u in range(UNROLL):
            k = base + u
            i = irow_ref[tile * slots + k]
            j = icol_ref[tile * slots + k]
            block = blocks_ref[0, k]
            at_i = jnp.concatenate([mine_ref[i], theirs_ref[i]], axis=0)
            at_j = jnp.concatenate([mine_ref[j], theirs_ref[j]], axis=0)
            direct = lax.dot_general(
                at_j, block, (((1,), (1,)), ((), ())), preferred_element_type=jnp.float32
            )
            mirrored = lax.dot_general(
                at_i, block, (((1,), (0,)), ((), ())), preferred_element_type=jnp.float32
            )
            terms.append((k < count, i, j, direct, mirrored))
        for used, i, j, direct, mirrored in terms:
            direct = jnp.where(used, direct, 0.0)
            mirrored = jnp.where(used, mirrored, 0.0)
            image_ref[i] += direct[:own]
            sum_ref[i] += direct[own:]
            image_ref[j] += mirrored[:own]
            sum_ref[j] += mirrored[own:]
        return carry

    lax.fori_loop(0, (count + UNROLL - 1) // UNROLL, group, 0)

    @pl.when(tile == pl.num_programs(0) - 1)
    def _():
        away_ref[...] = sum_ref[...].astype(away_ref.dtype)


def operate(blocks, irow, icol, count, mine, theirs):
    tiles, slots, width, _ = blocks.shape
    whole = pl.BlockSpec(mine.shape, lambda t, *_: (0, 0, 0))
    return pl.pallas_call(
        functools.partial(operate_kernel, slots),
        out_shape=(
            jax.ShapeDtypeStruct(mine.shape, jnp.float32),
            jax.ShapeDtypeStruct(mine.shape, jnp.bfloat16),
        ),
        grid_spec=pltpu.PrefetchScalarGridSpec(
            num_scalar_prefetch=3,
            grid=(tiles,),
            in_specs=[
                pl.BlockSpec((1, slots, width, width), lambda t, *_: (t, 0, 0, 0)),
                whole,
                whole,
            ],
            out_specs=(whole, whole),
            scratch_shapes=[pltpu.VMEM(mine.shape, jnp.float32)],
        ),
        compiler_params=pltpu.CompilerParams(vmem_limit_bytes=40 * 2**20),
        cost_estimate=pl.CostEstimate(
            flops=tiles * slots * width**3 * 4, bytes_accessed=60 * 2**20, transcendentals=0
        ),
    )(irow, icol, count, blocks, mine, theirs)


def by_columns(blocks, block_rows, block_cols, counts, diagonal, target):
    grid = ("row", "col")
    nrow, ncol = lax.axis_size("row"), lax.axis_size("col")
    devices = nrow * ncol
    stored = blocks[0, 0]
    slots, width, _ = stored.shape
    quarter = target.shape[0] // width
    own = target.shape[1] // devices
    row_blocks = ncol * quarter
    half = slots // 2
    row, col, core = lax.axis_index("row"), lax.axis_index("col"), lax.axis_index("rhs")

    irow = row * row_blocks + block_rows[0, 0]
    jcol = block_cols[0, 0]
    icol = (jcol // quarter * ncol + col) * quarter + jcol % quarter

    def every_other(index):
        return jnp.where(core == 0, index[0::2], index[1::2])

    used = (counts[0] - core + 1) // 2
    names = jnp.concatenate([every_other(irow), every_other(icol), used])
    names = jnp.pad(names, (0, -names.shape[0] % 1024)).reshape(-1, 128)
    diag_own = diagonal.reshape(quarter, width)
    target_blocks = target.reshape(quarter, width, target.shape[1])

    tiles, field, all_names, all_diag = spread(
        stored.reshape(half, 2, width, width), pack(target_blocks, devices), names, diag_own
    )
    all_names = all_names.reshape(devices, -1)
    irows = all_names[:, :half].reshape(-1)
    icols = all_names[:, half : 2 * half].reshape(-1)
    used = all_names[:, 2 * half]
    diag = all_diag.reshape(-1, 1, width)
    swap = [(0, 1), (1, 0)]

    def image_of(direction, low):
        theirs = lax.ppermute(low, "rhs", swap)
        here, away = operate(tiles, irows, icols, used, low, theirs)
        return diag * direction + here + lax.ppermute(away, "rhs", swap).astype(jnp.float32)

    def inner(a, b):
        return jnp.sum(a * b, axis=(0, 2), keepdims=True)

    def home(value):
        parcel = value.astype(jnp.bfloat16).reshape(devices, quarter, own, width)
        return lax.all_to_all(parcel, grid, split_axis=0, concat_axis=0, tiled=True)

    low = field.reshape(-1, own, width)
    start = low.astype(jnp.float32)
    norm0 = inner(start, start)
    image = image_of(start, low)
    alpha1 = norm0 / inner(start, image)
    first = start - alpha1 * image
    norm1 = inner(first, first)
    beta = norm1 / norm0
    direction = first + beta * start
    first_home = home(first)
    image = image_of(direction, direction.astype(jnp.bfloat16))
    alpha2 = norm1 / inner(direction, image)
    second = first - alpha2 * image
    second_home = home(second)
    scales = jnp.stack([alpha1, alpha2, beta]).reshape(1, 3, own)
    scales = lax.all_gather(scales, grid, axis=0, tiled=True)
    scales = scales.transpose(1, 0, 2).reshape(3, devices * own)
    answer, residual = finish(target_blocks, diag_own, first_home, second_home, scales)
    return (answer.reshape(target.shape), residual.reshape(target.shape))


def one_hot_slots(indices, valid, extent):
    return ((indices[None, :] == jnp.arange(extent)[:, None]) & valid[None, :]).astype(jnp.float32)


def on_device(blocks, block_rows, block_cols, counts, diagonal, target):
    highest = lax.Precision.HIGHEST
    nrow = lax.axis_size("row")
    ncol = lax.axis_size("col")
    tile_bytes = blocks[0, 0].size * blocks.dtype.itemsize
    if (
        nrow * ncol * tile_bytes <= GATHER_BYTES
        and ncol == 2
        and lax.axis_size("rhs") == 2
        and target.shape[1] == 16 * nrow * ncol
        and blocks.shape[2] % (2 * UNROLL) == 0
    ):
        return by_columns(blocks, block_rows, block_cols, counts, diagonal, target)
    stored = blocks[0, 0]
    slots = stored.shape[0]
    width = stored.shape[1]
    local = target.shape[0]
    ncols = target.shape[1]
    quarter = local // width
    row_blocks = ncol * quarter
    col_blocks = nrow * quarter
    valid = jnp.arange(slots) < counts[0, 0]
    rows_hot = one_hot_slots(block_rows[0, 0], valid, row_blocks)
    cols_hot = one_hot_slots(block_cols[0, 0], valid, col_blocks)

    def squares(vector):
        return lax.psum(jnp.sum(vector * vector, axis=0), ("row", "col"))

    solution = jnp.zeros_like(target)
    residual = target
    direction = target
    norm_now = squares(residual)
    for step in range(ITERS):
        operate_field_low = direction.astype(jnp.bfloat16)
        direct_gathered = lax.all_gather(operate_field_low, "row", axis=0, tiled=True).reshape(
            col_blocks, width, ncols
        )
        prod = jnp.einsum(
            "kab,kbc->kac",
            stored,
            direct_gathered[block_cols[0, 0]],
            preferred_element_type=jnp.float32,
        )
        direct_partial_value = jnp.einsum("ik,kac->iac", rows_hot, prod, precision=highest)
        direct = lax.psum_scatter(
            direct_partial_value.reshape(row_blocks * width, ncols).astype(jnp.bfloat16),
            "col",
            scatter_dimension=0,
            tiled=True,
        ).astype(jnp.float32)
        gathered = lax.all_gather(operate_field_low, "col", axis=0, tiled=True).reshape(
            row_blocks, width, ncols
        )
        tprod = jnp.einsum(
            "kba,kbc->kac", stored, gathered[block_rows[0, 0]], preferred_element_type=jnp.float32
        )
        partial_value = jnp.einsum("jk,kac->jac", cols_hot, tprod, precision=highest)
        parcel = partial_value.astype(jnp.bfloat16).reshape(nrow, local, ncols)
        mirrored = jnp.sum(
            lax.all_to_all(parcel, "row", split_axis=0, concat_axis=0, tiled=True).astype(
                jnp.float32
            ),
            axis=0,
        )
        image = diagonal[:, None] * direction + direct + mirrored
        curve = lax.psum(jnp.sum(direction * image, axis=0), ("row", "col"))
        alpha = norm_now / curve
        solution = solution + alpha * direction
        residual = residual - alpha * image
        if step + 1 < ITERS:
            norm_next = squares(residual)
            direction = residual + norm_next / norm_now * direction
            norm_now = norm_next
    return (solution, residual)


def solution(mesh):
    return jax.shard_map(
        on_device,
        mesh=mesh,
        in_specs=(
            P(("parts", "row"), "col", None, None, None),
            P(("parts", "row"), "col", None),
            P(("parts", "row"), "col", None),
            P(("parts", "row"), "col"),
            P(("parts", "row", "col")),
            P(("parts", "row", "col"), "rhs"),
        ),
        out_specs=(P(("parts", "row", "col"), "rhs"), P(("parts", "row", "col"), "rhs")),
        check_vma=False,
    )
```

```python
import functools
import jax
import jax.numpy as jnp
from jax import lax
from jax.experimental import pallas as pl
from jax.experimental.pallas import tpu as pltpu
from jax.sharding import PartitionSpec as P

ITERS = 2
UNROLL = 8
GATHER_BYTES = 32 * 2**20
MESH = pl.DeviceIdType.MESH
ANY = pl.BlockSpec(memory_space=pl.ANY)


def spread_kernel(
    nrow, stored, parcel, names, diag,
    tiles, field, all_names, all_diag,
    ring_send, ring_recv, send, recv, own_sem,
):
    devices = 2 * nrow
    row, col, core = lax.axis_index("row"), lax.axis_index("col"), lax.axis_index("rhs")
    me = row * 2 + col
    place = jnp.where(col == 0, row, devices - 1 - row)

    def device_at(place):
        place = lax.rem(place + devices, devices)
        back = place >= nrow
        return jnp.where(back, devices - 1 - place, place), jnp.where(back, 1, 0)

    def peer(offset):
        other = lax.rem(me + offset, devices)
        return {"row": other // 2, "col": lax.rem(other, 2)}

    barrier = pltpu.get_barrier_semaphore()
    for offset in range(1, devices):
        pl.semaphore_signal(barrier, inc=1, device_id=peer(offset), device_id_type=MESH)
    pl.semaphore_wait(barrier, devices - 1)

    half = tiles.shape[1]
    lanes = ring_send.shape[0]
    piece = half // lanes
    hops = []

    def hop(lane, step):
        way = lane % 2
        r, c = device_at(place + (1 if way == 0 else -1))
        if step == 0:
            source = stored.at[pl.ds(lane * piece, piece), core]
            origin = me
        else:
            orow, ocol = device_at(place + (-step if way == 0 else step))
            origin = orow * 2 + ocol
            source = tiles.at[origin, pl.ds(lane * piece, piece)]
        copy = pltpu.make_async_remote_copy(
            src_ref=source,
            dst_ref=tiles.at[origin, pl.ds(lane * piece, piece)],
            send_sem=ring_send.at[lane, step],
            recv_sem=ring_recv.at[lane, step],
            device_id={"row": r, "col": c},
            device_id_type=MESH,
        )
        copy.start()
        return copy

    now = [hop(lane, 0) for lane in range(lanes)]
    straight = []
    pairs = ((names, all_names, False), (diag, all_diag, False), (parcel, field, True))
    for n, (source, target, apart) in enumerate(pairs):
        for offset in range(1, devices):
            copy = pltpu.make_async_remote_copy(
                src_ref=source.at[lax.rem(me + offset, devices)] if apart else source,
                dst_ref=target.at[me],
                send_sem=send.at[n, offset - 1],
                recv_sem=recv.at[n, offset - 1],
                device_id=peer(offset),
                device_id_type=MESH,
            )
            copy.start()
            straight.append(copy)
    local = []
    owns = (
        (stored.at[:, core], tiles.at[me]),
        (names, all_names.at[me]),
        (diag, all_diag.at[me]),
        (parcel.at[me], field.at[me]),
    )
    for n, (source, target) in enumerate(owns):
        copy = pltpu.make_async_copy(source, target, own_sem.at[n])
        copy.start()
        local.append(copy)
    for step in range(1, devices):
        for lane in range(lanes):
            now[lane].wait_recv()
            if step < devices - 1:
                hops.append(now[lane])
                now[lane] = hop(lane, step)
    hops += now
    for copy in hops:
        copy.wait_send()
    for copy in straight:
        copy.wait()
    for copy in local:
        copy.wait()


def spread(stored, parcel, names, diag):
    nrow = lax.axis_size("row")
    devices = 2 * nrow
    half, cores, width, _ = stored.shape
    lanes = 6 if half % 6 == 0 else 2
    return pl.pallas_call(
        functools.partial(spread_kernel, nrow),
        out_shape=(
            jax.ShapeDtypeStruct((devices, half, width, width), stored.dtype),
            jax.ShapeDtypeStruct(parcel.shape, parcel.dtype),
            jax.ShapeDtypeStruct((devices,) + names.shape, names.dtype),
            jax.ShapeDtypeStruct((devices,) + diag.shape, diag.dtype),
        ),
        in_specs=[ANY] * 4,
        out_specs=[ANY] * 4,
        scratch_shapes=[
            pltpu.SemaphoreType.DMA((lanes, devices - 1)),
            pltpu.SemaphoreType.DMA((lanes, devices - 1)),
            pltpu.SemaphoreType.DMA((3, devices - 1)),
            pltpu.SemaphoreType.DMA((3, devices - 1)),
            pltpu.SemaphoreType.DMA((4,)),
        ],
        compiler_params=pltpu.CompilerParams(collective_id=0, has_side_effects=True),
    )(stored, parcel, names, diag)


def home_kernel(nrow, early, first, parcel, scale, late, field, scales, send, recv, own_sem):
    devices = 2 * nrow
    me = lax.axis_index("row") * 2 + lax.axis_index("col")

    def peer(offset):
        other = lax.rem(me + offset, devices)
        return {"row": other // 2, "col": lax.rem(other, 2)}

    barrier = pltpu.get_barrier_semaphore()
    for offset in range(1, devices):
        pl.semaphore_signal(barrier, inc=1, device_id=peer(offset), device_id_type=MESH)
    pl.semaphore_wait(barrier, devices - 1)
    copies = []
    rest = pl.ds(early, late.shape[1])
    for n, target in enumerate((scales, late, field)):
        for offset in range(1, devices):
            to = lax.rem(me + offset, devices)
            copy = pltpu.make_async_remote_copy(
                src_ref=(scale, first.at[to, rest], parcel.at[to])[n],
                dst_ref=target.at[me],
                send_sem=send.at[n, offset - 1],
                recv_sem=recv.at[n, offset - 1],
                device_id=peer(offset),
                device_id_type=MESH,
            )
            copy.start()
            copies.append(copy)
    owns = (
        (scale, scales.at[me]),
        (first.at[me, rest], late.at[me]),
        (parcel.at[me], field.at[me]),
    )
    for n, (source, target) in enumerate(owns):
        copy = pltpu.make_async_copy(source, target, own_sem.at[n])
        copy.start()
        copies.append(copy)
    for copy in copies:
        copy.wait()


def send_home(first, parcel, scale, early):
    nrow = lax.axis_size("row")
    devices, blocks = parcel.shape[:2]
    return pl.pallas_call(
        functools.partial(home_kernel, nrow, early),
        out_shape=(
            jax.ShapeDtypeStruct((devices, blocks - early) + parcel.shape[2:], parcel.dtype),
            jax.ShapeDtypeStruct(parcel.shape, parcel.dtype),
            jax.ShapeDtypeStruct((devices,) + scale.shape, scale.dtype),
        ),
        in_specs=[ANY] * 3,
        out_specs=[ANY] * 3,
        scratch_shapes=[
            pltpu.SemaphoreType.DMA((3, devices - 1)),
            pltpu.SemaphoreType.DMA((3, devices - 1)),
            pltpu.SemaphoreType.DMA((3,)),
        ],
        compiler_params=pltpu.CompilerParams(collective_id=1, has_side_effects=True),
    )(first, parcel, scale)


def pack_kernel(target_ref, parcel_ref):
    devices, blocks, own, width = parcel_ref.shape
    for b in range(blocks):
        low = target_ref[b].T.astype(jnp.bfloat16)
        parcel_ref[:, b] = low.reshape(devices, own, width)


def pack(target, devices):
    blocks, width, columns = target.shape
    own = columns // devices
    step = min(8, blocks)
    return pl.pallas_call(
        pack_kernel,
        out_shape=jax.ShapeDtypeStruct((devices, blocks, own, width), jnp.bfloat16),
        grid=(blocks // step,),
        in_specs=[pl.BlockSpec((step, width, columns), lambda g: (g, 0, 0))],
        out_specs=pl.BlockSpec((devices, step, own, width), lambda g: (0, g, 0, 0)),
    )(target)


def finish_kernel(me_ref, target_ref, diag_ref, early_ref, late_ref, second_ref, scale_ref,
                  answer_ref, residual_ref, first_ref):
    blocks, width, columns = target_ref.shape
    alpha1, alpha2, beta = scale_ref[0:1], scale_ref[1:2], scale_ref[2:3]
    devices = second_ref.shape[0]
    late = pl.program_id(0) >= pl.num_programs(0) // 2

    @pl.when(late)
    def _():
        first_ref[...] = late_ref[...]

    @pl.when(jnp.logical_not(late))
    def _():
        for source in range(devices):
            first_ref[source] = early_ref[lax.rem(me_ref[0] - source + devices, devices)]

    for b in range(blocks):
        target = target_ref[b]
        diag = jnp.transpose(jnp.broadcast_to(diag_ref[pl.ds(b, 1), :], (columns, width)))
        first = first_ref[:, b].reshape(columns, width).astype(jnp.float32).T
        second = second_ref[:, b].reshape(columns, width).astype(jnp.float32).T
        lost = target - target.astype(jnp.bfloat16).astype(jnp.float32)
        lost1 = lost - alpha1 * diag * lost
        answer_ref[b] = alpha1 * target + alpha2 * (first + lost1 + beta * target)
        residual_ref[b] = second + lost1 - alpha2 * diag * (lost1 + beta * lost)


def finish(me, target, diag, early, late, second, scales):
    blocks, width, columns = target.shape
    devices, _, own, _ = second.shape
    step = min(8, blocks // 2)
    last = blocks // step // 2
    whole = pl.BlockSpec((step, width, columns), lambda g: (g, 0, 0))
    part = pl.BlockSpec((devices, step, own, width), lambda g: (0, g, 0, 0))
    return pl.pallas_call(
        finish_kernel,
        out_shape=(jax.ShapeDtypeStruct(target.shape, jnp.float32),) * 2,
        grid=(blocks // step,),
        in_specs=[
            pl.BlockSpec(memory_space=pltpu.SMEM),
            whole,
            pl.BlockSpec((step, width), lambda g: (g, 0)),
            pl.BlockSpec((devices, step, own, width), lambda g: (0, jnp.minimum(g, last - 1), 0, 0)),
            pl.BlockSpec((devices, step, own, width), lambda g: (0, jnp.maximum(g - last, 0), 0, 0)),
            part,
            pl.BlockSpec(scales.shape, lambda g: (0, 0)),
        ],
        out_specs=(whole, whole),
        scratch_shapes=[pltpu.VMEM((devices, step, own, width), jnp.bfloat16)],
    )(me, target, diag, early, late, second, scales)


def operate_kernel(slots, irow_ref, icol_ref, count_ref, blocks_ref, mine_ref, theirs_ref,
                   image_ref, away_ref, sum_ref):
    tile = pl.program_id(0)
    own = mine_ref.shape[1]

    @pl.when(tile == 0)
    def _():
        image_ref[...] = jnp.zeros_like(image_ref)
        sum_ref[...] = jnp.zeros_like(sum_ref)

    count = count_ref[tile]

    def group(step, carry):
        base = step * UNROLL
        terms = []
        for u in range(UNROLL):
            k = base + u
            i = irow_ref[tile * slots + k]
            j = icol_ref[tile * slots + k]
            block = blocks_ref[0, k]
            at_i = jnp.concatenate([mine_ref[i], theirs_ref[i]], axis=0)
            at_j = jnp.concatenate([mine_ref[j], theirs_ref[j]], axis=0)
            direct = lax.dot_general(
                at_j, block, (((1,), (1,)), ((), ())), preferred_element_type=jnp.float32
            )
            mirrored = lax.dot_general(
                at_i, block, (((1,), (0,)), ((), ())), preferred_element_type=jnp.float32
            )
            terms.append((k < count, i, j, direct, mirrored))
        for used, i, j, direct, mirrored in terms:
            direct = jnp.where(used, direct, 0.0)
            mirrored = jnp.where(used, mirrored, 0.0)
            image_ref[i] += direct[:own]
            sum_ref[i] += direct[own:]
            image_ref[j] += mirrored[:own]
            sum_ref[j] += mirrored[own:]
        return carry

    lax.fori_loop(0, (count + UNROLL - 1) // UNROLL, group, 0)

    @pl.when(tile == pl.num_programs(0) - 1)
    def _():
        away_ref[...] = sum_ref[...].astype(away_ref.dtype)


def operate(blocks, irow, icol, count, mine, theirs):
    tiles, slots, width, _ = blocks.shape
    whole = pl.BlockSpec(mine.shape, lambda t, *_: (0, 0, 0))
    return pl.pallas_call(
        functools.partial(operate_kernel, slots),
        out_shape=(
            jax.ShapeDtypeStruct(mine.shape, jnp.float32),
            jax.ShapeDtypeStruct(mine.shape, jnp.bfloat16),
        ),
        grid_spec=pltpu.PrefetchScalarGridSpec(
            num_scalar_prefetch=3,
            grid=(tiles,),
            in_specs=[
                pl.BlockSpec((1, slots, width, width), lambda t, *_: (t, 0, 0, 0)),
                whole,
                whole,
            ],
            out_specs=(whole, whole),
            scratch_shapes=[pltpu.VMEM(mine.shape, jnp.float32)],
        ),
        compiler_params=pltpu.CompilerParams(vmem_limit_bytes=40 * 2**20),
        cost_estimate=pl.CostEstimate(
            flops=tiles * slots * width**3 * 4, bytes_accessed=60 * 2**20, transcendentals=0
        ),
    )(irow, icol, count, blocks, mine, theirs)


def by_columns(blocks, block_rows, block_cols, counts, diagonal, target):
    grid = ("row", "col")
    nrow, ncol = lax.axis_size("row"), lax.axis_size("col")
    devices = nrow * ncol
    stored = blocks[0, 0]
    slots, width, _ = stored.shape
    quarter = target.shape[0] // width
    own = target.shape[1] // devices
    row_blocks = ncol * quarter
    half = slots // 2
    row, col, core = lax.axis_index("row"), lax.axis_index("col"), lax.axis_index("rhs")

    irow = row * row_blocks + block_rows[0, 0]
    jcol = block_cols[0, 0]
    icol = (jcol // quarter * ncol + col) * quarter + jcol % quarter

    def every_other(index):
        return jnp.where(core == 0, index[0::2], index[1::2])

    used = (counts[0] - core + 1) // 2
    names = jnp.concatenate([every_other(irow), every_other(icol), used])
    names = jnp.pad(names, (0, -names.shape[0] % 1024)).reshape(-1, 128)
    diag_own = diagonal.reshape(quarter, width)
    target_blocks = target.reshape(quarter, width, target.shape[1])

    tiles, field, all_names, all_diag = spread(
        stored.reshape(half, 2, width, width), pack(target_blocks, devices), names, diag_own
    )
    all_names = all_names.reshape(devices, -1)
    irows = all_names[:, :half].reshape(-1)
    icols = all_names[:, half : 2 * half].reshape(-1)
    used = all_names[:, 2 * half]
    diag = all_diag.reshape(-1, 1, width)
    swap = [(0, 1), (1, 0)]

    def image_of(direction, low, beside=()):
        theirs = lax.ppermute(low, "rhs", swap)
        here, away = operate(tiles, irows, icols, used, low, theirs)
        (here, away), beside = lax.optimization_barrier(((here, away), beside))
        away = lax.ppermute(away, "rhs", swap).astype(jnp.float32)
        return diag * direction + here + away, beside

    def inner(a, b):
        return jnp.sum(a * b, axis=(0, 2), keepdims=True)

    me = row * ncol + col

    def parcels(value):
        return value.astype(jnp.bfloat16).reshape(devices, quarter, own, width)

    def home_by_offset(parcel):
        pieces = []
        for offset in range(devices):
            piece = lax.dynamic_index_in_dim(parcel, (me + offset) % devices, 0, keepdims=False)
            if offset:
                pairs = [(d, (d + offset) % devices) for d in range(devices)]
                piece = lax.ppermute(piece, grid, pairs)
            pieces.append(piece)
        return pieces

    low = field.reshape(-1, own, width)
    start = low.astype(jnp.float32)
    norm0 = inner(start, start)
    image, _ = image_of(start, low)
    alpha1 = norm0 / inner(start, image)
    first = start - alpha1 * image
    norm1 = inner(first, first)
    beta = norm1 / norm0
    direction = first + beta * start
    first_parcel = parcels(first)
    early = quarter // 2
    pieces = home_by_offset(first_parcel[:, :early])
    image, pieces = image_of(direction, direction.astype(jnp.bfloat16), pieces)
    first_early = jnp.stack(pieces)
    alpha2 = norm1 / inner(direction, image)
    second = first - alpha2 * image
    scale = jnp.stack([alpha1, alpha2, beta]).reshape(3, own)
    scale = jnp.pad(scale, ((0, 5), (0, 128 - own)))
    first_late, second_home, scales = send_home(first_parcel, parcels(second), scale, early)
    scales = scales[:, :3, :own]
    scales = scales.transpose(1, 0, 2).reshape(3, devices * own)
    answer, residual = finish(
        me.reshape(1), target_blocks, diag_own, first_early, first_late, second_home, scales
    )
    return (answer.reshape(target.shape), residual.reshape(target.shape))


def one_hot_slots(indices, valid, extent):
    return ((indices[None, :] == jnp.arange(extent)[:, None]) & valid[None, :]).astype(jnp.float32)


def on_device(blocks, block_rows, block_cols, counts, diagonal, target):
    highest = lax.Precision.HIGHEST
    nrow = lax.axis_size("row")
    ncol = lax.axis_size("col")
    tile_bytes = blocks[0, 0].size * blocks.dtype.itemsize
    if (
        nrow * ncol * tile_bytes <= GATHER_BYTES
        and ncol == 2
        and lax.axis_size("rhs") == 2
        and target.shape[1] == 16 * nrow * ncol
        and blocks.shape[2] % (2 * UNROLL) == 0
        and target.shape[0] // blocks.shape[3] % 16 == 0
    ):
        return by_columns(blocks, block_rows, block_cols, counts, diagonal, target)
    stored = blocks[0, 0]
    slots = stored.shape[0]
    width = stored.shape[1]
    local = target.shape[0]
    ncols = target.shape[1]
    quarter = local // width
    row_blocks = ncol * quarter
    col_blocks = nrow * quarter
    valid = jnp.arange(slots) < counts[0, 0]
    rows_hot = one_hot_slots(block_rows[0, 0], valid, row_blocks)
    cols_hot = one_hot_slots(block_cols[0, 0], valid, col_blocks)

    def squares(vector):
        return lax.psum(jnp.sum(vector * vector, axis=0), ("row", "col"))

    solution = jnp.zeros_like(target)
    residual = target
    direction = target
    norm_now = squares(residual)
    for step in range(ITERS):
        operate_field_low = direction.astype(jnp.bfloat16)
        direct_gathered = lax.all_gather(operate_field_low, "row", axis=0, tiled=True).reshape(
            col_blocks, width, ncols
        )
        prod = jnp.einsum(
            "kab,kbc->kac",
            stored,
            direct_gathered[block_cols[0, 0]],
            preferred_element_type=jnp.float32,
        )
        direct_partial_value = jnp.einsum("ik,kac->iac", rows_hot, prod, precision=highest)
        direct = lax.psum_scatter(
            direct_partial_value.reshape(row_blocks * width, ncols).astype(jnp.bfloat16),
            "col",
            scatter_dimension=0,
            tiled=True,
        ).astype(jnp.float32)
        gathered = lax.all_gather(operate_field_low, "col", axis=0, tiled=True).reshape(
            row_blocks, width, ncols
        )
        tprod = jnp.einsum(
            "kba,kbc->kac", stored, gathered[block_rows[0, 0]], preferred_element_type=jnp.float32
        )
        partial_value = jnp.einsum("jk,kac->jac", cols_hot, tprod, precision=highest)
        parcel = partial_value.astype(jnp.bfloat16).reshape(nrow, local, ncols)
        mirrored = jnp.sum(
            lax.all_to_all(parcel, "row", split_axis=0, concat_axis=0, tiled=True).astype(
                jnp.float32
            ),
            axis=0,
        )
        image = diagonal[:, None] * direction + direct + mirrored
        curve = lax.psum(jnp.sum(direction * image, axis=0), ("row", "col"))
        alpha = norm_now / curve
        solution = solution + alpha * direction
        residual = residual - alpha * image
        if step + 1 < ITERS:
            norm_next = squares(residual)
            direction = residual + norm_next / norm_now * direction
            norm_now = norm_next
    return (solution, residual)


def solution(mesh):
    return jax.shard_map(
        on_device,
        mesh=mesh,
        in_specs=(
            P(("parts", "row"), "col", None, None, None),
            P(("parts", "row"), "col", None),
            P(("parts", "row"), "col", None),
            P(("parts", "row"), "col"),
            P(("parts", "row", "col")),
            P(("parts", "row", "col"), "rhs"),
        ),
        out_specs=(P(("parts", "row", "col"), "rhs"), P(("parts", "row", "col"), "rhs")),
        check_vma=False,
    )
```

```python
import functools
import jax
import jax.numpy as jnp
from jax import lax
from jax.experimental import pallas as pl
from jax.experimental.pallas import tpu as pltpu
from jax.sharding import PartitionSpec as P

ITERS = 2
UNROLL = 8
GATHER_BYTES = 32 * 2**20
MESH = pl.DeviceIdType.MESH
ANY = pl.BlockSpec(memory_space=pl.ANY)


def flipped(index, bits, devices):
    total, unit = index, 1
    while unit < devices:
        if bits & unit:
            total = total + unit * (1 - 2 * lax.rem(index // unit, 2))
        unit *= 2
    return total


def spread_kernel(
    nrow, stored, target, names, diag,
    tiles, field, all_names, all_diag,
    parcel, ring_send, ring_recv, send, recv, own_sem,
):
    devices = 2 * nrow
    row, col, core = lax.axis_index("row"), lax.axis_index("col"), lax.axis_index("rhs")
    me = row * 2 + col
    place = jnp.where(col == 0, row, devices - 1 - row)

    def device_at(place):
        place = lax.rem(place + devices, devices)
        back = place >= nrow
        return jnp.where(back, devices - 1 - place, place), jnp.where(back, 1, 0)

    def peer(offset):
        other = lax.rem(me + offset, devices)
        return {"row": other // 2, "col": lax.rem(other, 2)}

    barrier = pltpu.get_barrier_semaphore()
    for offset in range(1, devices):
        pl.semaphore_signal(barrier, inc=1, device_id=peer(offset), device_id_type=MESH)
    pl.semaphore_wait(barrier, devices - 1)

    half = tiles.shape[1]
    lanes = ring_send.shape[0]
    piece = half // lanes
    hops = []

    def hop(lane, step):
        way = lane % 2
        r, c = device_at(place + (1 if way == 0 else -1))
        if step == 0:
            source = stored.at[pl.ds(lane * piece, piece), core]
            origin = me
        else:
            orow, ocol = device_at(place + (-step if way == 0 else step))
            origin = orow * 2 + ocol
            source = tiles.at[origin, pl.ds(lane * piece, piece)]
        copy = pltpu.make_async_remote_copy(
            src_ref=source,
            dst_ref=tiles.at[origin, pl.ds(lane * piece, piece)],
            send_sem=ring_send.at[lane, step],
            recv_sem=ring_recv.at[lane, step],
            device_id={"row": r, "col": c},
            device_id_type=MESH,
        )
        copy.start()
        return copy

    now = [hop(lane, 0) for lane in range(lanes)]

    def pack(b, carry):
        low = target[b].astype(jnp.bfloat16).T
        parcel[:, b] = low.reshape(devices, parcel.shape[2], parcel.shape[3])
        return carry

    lax.fori_loop(0, target.shape[0], pack, 0)
    straight = []
    pairs = ((names, all_names, False), (diag, all_diag, False), (parcel, field, True))
    for n, (source, whole, apart) in enumerate(pairs):
        for offset in range(1, devices):
            copy = pltpu.make_async_remote_copy(
                src_ref=source.at[lax.rem(me + offset, devices)] if apart else source,
                dst_ref=whole.at[me],
                send_sem=send.at[n, offset - 1],
                recv_sem=recv.at[n, offset - 1],
                device_id=peer(offset),
                device_id_type=MESH,
            )
            copy.start()
            straight.append(copy)
    local = []
    owns = (
        (stored.at[:, core], tiles.at[me]),
        (names, all_names.at[me]),
        (diag, all_diag.at[me]),
        (parcel.at[me], field.at[me]),
    )
    for n, (source, whole) in enumerate(owns):
        copy = pltpu.make_async_copy(source, whole, own_sem.at[n])
        copy.start()
        local.append(copy)
    for step in range(1, devices):
        for lane in range(lanes):
            now[lane].wait_recv()
            if step < devices - 1:
                hops.append(now[lane])
                now[lane] = hop(lane, step)
    hops += now
    for copy in hops:
        copy.wait_send()
    for copy in straight:
        copy.wait()
    for copy in local:
        copy.wait()


def spread(stored, target, names, diag):
    nrow = lax.axis_size("row")
    devices = 2 * nrow
    half, cores, width, _ = stored.shape
    parcel = (devices, target.shape[0], target.shape[2] // devices, target.shape[1])
    lanes = 6 if half % 6 == 0 else 2
    return pl.pallas_call(
        functools.partial(spread_kernel, nrow),
        out_shape=(
            jax.ShapeDtypeStruct((devices, half, width, width), stored.dtype),
            jax.ShapeDtypeStruct(parcel, jnp.bfloat16),
            jax.ShapeDtypeStruct((devices,) + names.shape, names.dtype),
            jax.ShapeDtypeStruct((devices,) + diag.shape, diag.dtype),
        ),
        in_specs=[ANY, pl.BlockSpec(memory_space=pltpu.VMEM), ANY, ANY],
        out_specs=[ANY] * 4,
        scratch_shapes=[
            pltpu.VMEM(parcel, jnp.bfloat16),
            pltpu.SemaphoreType.DMA((lanes, devices - 1)),
            pltpu.SemaphoreType.DMA((lanes, devices - 1)),
            pltpu.SemaphoreType.DMA((3, devices - 1)),
            pltpu.SemaphoreType.DMA((3, devices - 1)),
            pltpu.SemaphoreType.DMA((4,)),
        ],
        compiler_params=pltpu.CompilerParams(collective_id=0, has_side_effects=True),
    )(stored, target, names, diag)


def home_kernel(nrow, early, first, parcel, scale, late, field, scales, send, recv, own_sem):
    devices = 2 * nrow
    me = lax.axis_index("row") * 2 + lax.axis_index("col")

    def peer(bits):
        other = flipped(me, bits, devices)
        return {"row": other // 2, "col": lax.rem(other, 2)}

    barrier = pltpu.get_barrier_semaphore()
    for offset in range(1, devices):
        pl.semaphore_signal(barrier, inc=1, device_id=peer(offset), device_id_type=MESH)
    pl.semaphore_wait(barrier, devices - 1)
    copies = []
    rest = pl.ds(early, late.shape[1] - early)
    for n in range(3):
        for offset in range(1, devices):
            to = flipped(me, offset, devices)
            if n == 0:
                source, target = scale, scales.at[me]
            elif n == 2:
                source, target = parcel.at[to], field.at[me]
            elif offset < devices // 2:
                source, target = first.at[to], late.at[me]
            else:
                source, target = first.at[to, rest], late.at[me, rest]
            copy = pltpu.make_async_remote_copy(
                src_ref=source,
                dst_ref=target,
                send_sem=send.at[n, offset - 1],
                recv_sem=recv.at[n, offset - 1],
                device_id=peer(offset),
                device_id_type=MESH,
            )
            copy.start()
            copies.append(copy)
    owns = (
        (scale, scales.at[me]),
        (first.at[me], late.at[me]),
        (parcel.at[me], field.at[me]),
    )
    for n, (source, target) in enumerate(owns):
        copy = pltpu.make_async_copy(source, target, own_sem.at[n])
        copy.start()
        copies.append(copy)
    for copy in copies:
        copy.wait()


def send_home(first, parcel, scale, early):
    nrow = lax.axis_size("row")
    devices = parcel.shape[0]
    return pl.pallas_call(
        functools.partial(home_kernel, nrow, early),
        out_shape=(
            jax.ShapeDtypeStruct(parcel.shape, parcel.dtype),
            jax.ShapeDtypeStruct(parcel.shape, parcel.dtype),
            jax.ShapeDtypeStruct((devices,) + scale.shape, scale.dtype),
        ),
        in_specs=[ANY] * 3,
        out_specs=[ANY] * 3,
        scratch_shapes=[
            pltpu.SemaphoreType.DMA((3, devices - 1)),
            pltpu.SemaphoreType.DMA((3, devices - 1)),
            pltpu.SemaphoreType.DMA((3,)),
        ],
        compiler_params=pltpu.CompilerParams(collective_id=1, has_side_effects=True),
    )(first, parcel, scale)


def finish_kernel(me_ref, target_ref, diag_ref, early_ref, late_ref, second_ref, scale_ref,
                  answer_ref, residual_ref, first_ref):
    blocks, width, columns = target_ref.shape
    alpha1, alpha2, beta = scale_ref[0:1], scale_ref[1:2], scale_ref[2:3]
    devices = second_ref.shape[0]
    first_ref[...] = late_ref[...]

    @pl.when(pl.program_id(0) < pl.num_programs(0) // 2)
    def _():
        for far in range(devices // 2):
            first_ref[me_ref[0] ^ (devices // 2 + far)] = early_ref[far]

    diags = diag_ref[...].T
    for b in range(blocks):
        target = target_ref[b]
        diag = diags[:, b : b + 1]
        first = first_ref[:, b].reshape(columns, width).T.astype(jnp.float32)
        second = second_ref[:, b].reshape(columns, width).T.astype(jnp.float32)
        lost = target - target.astype(jnp.bfloat16).astype(jnp.float32)
        lost1 = lost - alpha1 * diag * lost
        answer_ref[b] = alpha1 * target + alpha2 * (first + lost1 + beta * target)
        residual_ref[b] = second + lost1 - alpha2 * diag * (lost1 + beta * lost)


def finish(me, target, diag, early, late, second, scales):
    blocks, width, columns = target.shape
    devices, _, own, _ = second.shape
    step = min(8, blocks // 2)
    last = blocks // step // 2
    whole = pl.BlockSpec((step, width, columns), lambda g: (g, 0, 0))
    part = pl.BlockSpec((devices, step, own, width), lambda g: (0, g, 0, 0))
    return pl.pallas_call(
        finish_kernel,
        out_shape=(jax.ShapeDtypeStruct(target.shape, jnp.float32),) * 2,
        grid=(blocks // step,),
        in_specs=[
            pl.BlockSpec(memory_space=pltpu.SMEM),
            whole,
            pl.BlockSpec((step, width), lambda g: (g, 0)),
            pl.BlockSpec(early.shape[:1] + (step, own, width), lambda g: (0, jnp.minimum(g, last - 1), 0, 0)),
            part,
            part,
            pl.BlockSpec(scales.shape, lambda g: (0, 0)),
        ],
        out_specs=(whole, whole),
        scratch_shapes=[pltpu.VMEM((devices, step, own, width), jnp.bfloat16)],
    )(me, target, diag, early, late, second, scales)


def operate_kernel(slots, irow_ref, icol_ref, count_ref, blocks_ref, mine_ref, theirs_ref,
                   image_ref, away_ref, sum_ref):
    tile = pl.program_id(0)
    own = mine_ref.shape[1]

    @pl.when(tile == 0)
    def _():
        image_ref[...] = jnp.zeros_like(image_ref)
        sum_ref[...] = jnp.zeros_like(sum_ref)

    count = count_ref[tile]

    def group(step, carry):
        base = step * UNROLL
        terms = []
        for u in range(UNROLL):
            k = base + u
            i = irow_ref[tile * slots + k]
            j = icol_ref[tile * slots + k]
            block = blocks_ref[0, k]
            at_i = jnp.concatenate([mine_ref[i], theirs_ref[i]], axis=0)
            at_j = jnp.concatenate([mine_ref[j], theirs_ref[j]], axis=0)
            direct = lax.dot_general(
                at_j, block, (((1,), (1,)), ((), ())), preferred_element_type=jnp.float32
            )
            mirrored = lax.dot_general(
                at_i, block, (((1,), (0,)), ((), ())), preferred_element_type=jnp.float32
            )
            terms.append((k < count, i, j, direct, mirrored))
        for used, i, j, direct, mirrored in terms:
            direct = jnp.where(used, direct, 0.0)
            mirrored = jnp.where(used, mirrored, 0.0)
            image_ref[i] += direct[:own]
            sum_ref[i] += direct[own:]
            image_ref[j] += mirrored[:own]
            sum_ref[j] += mirrored[own:]
        return carry

    lax.fori_loop(0, (count + UNROLL - 1) // UNROLL, group, 0)

    @pl.when(tile == pl.num_programs(0) - 1)
    def _():
        away_ref[...] = sum_ref[...].astype(away_ref.dtype)


def operate(blocks, irow, icol, count, mine, theirs):
    tiles, slots, width, _ = blocks.shape
    whole = pl.BlockSpec(mine.shape, lambda t, *_: (0, 0, 0))
    return pl.pallas_call(
        functools.partial(operate_kernel, slots),
        out_shape=(
            jax.ShapeDtypeStruct(mine.shape, jnp.float32),
            jax.ShapeDtypeStruct(mine.shape, jnp.bfloat16),
        ),
        grid_spec=pltpu.PrefetchScalarGridSpec(
            num_scalar_prefetch=3,
            grid=(tiles,),
            in_specs=[
                pl.BlockSpec((1, slots, width, width), lambda t, *_: (t, 0, 0, 0)),
                whole,
                whole,
            ],
            out_specs=(whole, whole),
            scratch_shapes=[pltpu.VMEM(mine.shape, jnp.float32)],
        ),
        compiler_params=pltpu.CompilerParams(vmem_limit_bytes=40 * 2**20),
        cost_estimate=pl.CostEstimate(
            flops=tiles * slots * width**3 * 4, bytes_accessed=60 * 2**20, transcendentals=0
        ),
    )(irow, icol, count, blocks, mine, theirs)


def by_columns(blocks, block_rows, block_cols, counts, diagonal, target):
    grid = ("row", "col")
    nrow, ncol = lax.axis_size("row"), lax.axis_size("col")
    devices = nrow * ncol
    stored = blocks[0, 0]
    slots, width, _ = stored.shape
    quarter = target.shape[0] // width
    own = target.shape[1] // devices
    row_blocks = ncol * quarter
    half = slots // 2
    row, col, core = lax.axis_index("row"), lax.axis_index("col"), lax.axis_index("rhs")

    irow = row * row_blocks + block_rows[0, 0]
    jcol = block_cols[0, 0]
    icol = (jcol // quarter * ncol + col) * quarter + jcol % quarter

    def every_other(index):
        return jnp.where(core == 0, index[0::2], index[1::2])

    used = (counts[0] - core + 1) // 2
    names = jnp.concatenate([every_other(irow), every_other(icol), used])
    names = jnp.pad(names, (0, -names.shape[0] % 1024)).reshape(-1, 128)
    diag_own = diagonal.reshape(quarter, width)
    target_blocks = target.reshape(quarter, width, target.shape[1])

    tiles, field, all_names, all_diag = spread(
        stored.reshape(half, 2, width, width), target_blocks, names, diag_own
    )
    all_names = all_names.reshape(devices, -1)
    irows = all_names[:, :half].reshape(-1)
    icols = all_names[:, half : 2 * half].reshape(-1)
    used = all_names[:, 2 * half]
    diag = all_diag.reshape(-1, 1, width)
    swap = [(0, 1), (1, 0)]

    def image_of(direction, low, beside=()):
        theirs = lax.ppermute(low, "rhs", swap)
        here, away = operate(tiles, irows, icols, used, low, theirs)
        (here, away), beside = lax.optimization_barrier(((here, away), beside))
        away = lax.ppermute(away, "rhs", swap).astype(jnp.float32)
        return diag * direction + here + away, beside

    def inner(a, b):
        return jnp.sum(a * b, axis=(0, 2), keepdims=True)

    me = row * ncol + col

    def parcels(value):
        return value.astype(jnp.bfloat16).reshape(devices, quarter, own, width)

    def far_home(parcel):
        pieces = []
        for bits in range(devices // 2, devices):
            piece = lax.dynamic_index_in_dim(parcel, me ^ bits, 0, keepdims=False)
            pieces.append(lax.ppermute(piece, grid, [(d, d ^ bits) for d in range(devices)]))
        return pieces

    low = field.reshape(-1, own, width)
    start = low.astype(jnp.float32)
    norm0 = inner(start, start)
    image, _ = image_of(start, low)
    alpha1 = norm0 / inner(start, image)
    first = start - alpha1 * image
    norm1 = inner(first, first)
    beta = norm1 / norm0
    direction = first + beta * start
    first_parcel = parcels(first)
    early = quarter // 2
    pieces = far_home(first_parcel[:, :early])
    image, pieces = image_of(direction, direction.astype(jnp.bfloat16), pieces)
    first_early = jnp.stack(pieces)
    alpha2 = norm1 / inner(direction, image)
    second = first - alpha2 * image
    scale = jnp.stack([alpha1, alpha2, beta]).reshape(3, own)
    scale = jnp.pad(scale, ((0, 5), (0, 128 - own)))
    first_late, second_home, scales = send_home(first_parcel, parcels(second), scale, early)
    scales = scales[:, :3, :own]
    scales = scales.transpose(1, 0, 2).reshape(3, devices * own)
    answer, residual = finish(
        me.reshape(1), target_blocks, diag_own, first_early, first_late, second_home, scales
    )
    return (answer.reshape(target.shape), residual.reshape(target.shape))


def one_hot_slots(indices, valid, extent):
    return ((indices[None, :] == jnp.arange(extent)[:, None]) & valid[None, :]).astype(jnp.float32)


def on_device(blocks, block_rows, block_cols, counts, diagonal, target):
    highest = lax.Precision.HIGHEST
    nrow = lax.axis_size("row")
    ncol = lax.axis_size("col")
    tile_bytes = blocks[0, 0].size * blocks.dtype.itemsize
    if (
        nrow * ncol * tile_bytes <= GATHER_BYTES
        and ncol == 2
        and nrow & (nrow - 1) == 0
        and lax.axis_size("rhs") == 2
        and target.shape[1] == 16 * nrow * ncol
        and blocks.shape[2] % (2 * UNROLL) == 0
        and target.shape[0] // blocks.shape[3] % 16 == 0
    ):
        return by_columns(blocks, block_rows, block_cols, counts, diagonal, target)
    stored = blocks[0, 0]
    slots = stored.shape[0]
    width = stored.shape[1]
    local = target.shape[0]
    ncols = target.shape[1]
    quarter = local // width
    row_blocks = ncol * quarter
    col_blocks = nrow * quarter
    valid = jnp.arange(slots) < counts[0, 0]
    rows_hot = one_hot_slots(block_rows[0, 0], valid, row_blocks)
    cols_hot = one_hot_slots(block_cols[0, 0], valid, col_blocks)

    def squares(vector):
        return lax.psum(jnp.sum(vector * vector, axis=0), ("row", "col"))

    solution = jnp.zeros_like(target)
    residual = target
    direction = target
    norm_now = squares(residual)
    for step in range(ITERS):
        operate_field_low = direction.astype(jnp.bfloat16)
        direct_gathered = lax.all_gather(operate_field_low, "row", axis=0, tiled=True).reshape(
            col_blocks, width, ncols
        )
        prod = jnp.einsum(
            "kab,kbc->kac",
            stored,
            direct_gathered[block_cols[0, 0]],
            preferred_element_type=jnp.float32,
        )
        direct_partial_value = jnp.einsum("ik,kac->iac", rows_hot, prod, precision=highest)
        direct = lax.psum_scatter(
            direct_partial_value.reshape(row_blocks * width, ncols).astype(jnp.bfloat16),
            "col",
            scatter_dimension=0,
            tiled=True,
        ).astype(jnp.float32)
        gathered = lax.all_gather(operate_field_low, "col", axis=0, tiled=True).reshape(
            row_blocks, width, ncols
        )
        tprod = jnp.einsum(
            "kba,kbc->kac", stored, gathered[block_rows[0, 0]], preferred_element_type=jnp.float32
        )
        partial_value = jnp.einsum("jk,kac->jac", cols_hot, tprod, precision=highest)
        parcel = partial_value.astype(jnp.bfloat16).reshape(nrow, local, ncols)
        mirrored = jnp.sum(
            lax.all_to_all(parcel, "row", split_axis=0, concat_axis=0, tiled=True).astype(
                jnp.float32
            ),
            axis=0,
        )
        image = diagonal[:, None] * direction + direct + mirrored
        curve = lax.psum(jnp.sum(direction * image, axis=0), ("row", "col"))
        alpha = norm_now / curve
        solution = solution + alpha * direction
        residual = residual - alpha * image
        if step + 1 < ITERS:
            norm_next = squares(residual)
            direction = residual + norm_next / norm_now * direction
            norm_now = norm_next
    return (solution, residual)


def solution(mesh):
    return jax.shard_map(
        on_device,
        mesh=mesh,
        in_specs=(
            P(("parts", "row"), "col", None, None, None),
            P(("parts", "row"), "col", None),
            P(("parts", "row"), "col", None),
            P(("parts", "row"), "col"),
            P(("parts", "row", "col")),
            P(("parts", "row", "col"), "rhs"),
        ),
        out_specs=(P(("parts", "row", "col"), "rhs"), P(("parts", "row", "col"), "rhs")),
        check_vma=False,
    )
```

```python
import functools
import jax
import jax.numpy as jnp
from jax import lax
from jax.experimental import pallas as pl
from jax.experimental.pallas import tpu as pltpu
from jax.sharding import PartitionSpec as P

ITERS = 2
UNROLL = 8
GATHER_BYTES = 32 * 2**20
MESH = pl.DeviceIdType.MESH
ANY = pl.BlockSpec(memory_space=pl.ANY)


def flipped(index, bits, devices):
    total, unit = index, 1
    while unit < devices:
        if bits & unit:
            total = total + unit * (1 - 2 * lax.rem(index // unit, 2))
        unit *= 2
    return total


def spread_kernel(
    nrow, stored, target, names, diag,
    tiles, field, theirs, all_names, all_diag,
    parcel, ring_send, ring_recv, send, recv, own_sem, pair_sem,
):
    devices = 2 * nrow
    row, col, core = lax.axis_index("row"), lax.axis_index("col"), lax.axis_index("rhs")
    me = row * 2 + col
    place = jnp.where(col == 0, row, devices - 1 - row)

    def device_at(place):
        place = lax.rem(place + devices, devices)
        back = place >= nrow
        return jnp.where(back, devices - 1 - place, place), jnp.where(back, 1, 0)

    def peer(offset):
        other = lax.rem(me + offset, devices)
        return {"row": other // 2, "col": lax.rem(other, 2)}

    barrier = pltpu.get_barrier_semaphore()
    for offset in range(1, devices):
        pl.semaphore_signal(barrier, inc=1, device_id=peer(offset), device_id_type=MESH)
    sibling = {"rhs": 1 - core}
    pl.semaphore_signal(barrier, inc=1, device_id=sibling, device_id_type=MESH)
    pl.semaphore_wait(barrier, devices)

    half = tiles.shape[1]
    lanes = ring_send.shape[0]
    piece = half // lanes
    hops = []

    def hop(lane, step):
        way = lane % 2
        r, c = device_at(place + (1 if way == 0 else -1))
        if step == 0:
            source = stored.at[pl.ds(lane * piece, piece), core]
            origin = me
        else:
            orow, ocol = device_at(place + (-step if way == 0 else step))
            origin = orow * 2 + ocol
            source = tiles.at[origin, pl.ds(lane * piece, piece)]
        copy = pltpu.make_async_remote_copy(
            src_ref=source,
            dst_ref=tiles.at[origin, pl.ds(lane * piece, piece)],
            send_sem=ring_send.at[lane, step],
            recv_sem=ring_recv.at[lane, step],
            device_id={"row": r, "col": c},
            device_id_type=MESH,
        )
        copy.start()
        return copy

    now = [hop(lane, 0) for lane in range(lanes)]

    def pack(b, carry):
        low = target[b].astype(jnp.bfloat16).T
        parcel[:, b] = low.reshape(devices, parcel.shape[2], parcel.shape[3])
        return carry

    lax.fori_loop(0, target.shape[0], pack, 0)
    straight = []
    pairs = ((names, all_names, False), (diag, all_diag, False), (parcel, field, True))
    for n, (source, whole, apart) in enumerate(pairs):
        for offset in range(1, devices):
            copy = pltpu.make_async_remote_copy(
                src_ref=source.at[lax.rem(me + offset, devices)] if apart else source,
                dst_ref=whole.at[me],
                send_sem=send.at[n, offset - 1],
                recv_sem=recv.at[n, offset - 1],
                device_id=peer(offset),
                device_id_type=MESH,
            )
            copy.start()
            straight.append(copy)
    local = []
    owns = (
        (stored.at[:, core], tiles.at[me]),
        (names, all_names.at[me]),
        (diag, all_diag.at[me]),
        (parcel.at[me], field.at[me]),
    )
    for n, (source, whole) in enumerate(owns):
        copy = pltpu.make_async_copy(source, whole, own_sem.at[n])
        copy.start()
        local.append(copy)
    for step in range(1, devices):
        if step == devices - 1:
            for copy in straight:
                copy.wait()
            for copy in local:
                copy.wait()
            pair = pltpu.make_async_remote_copy(
                src_ref=field,
                dst_ref=theirs,
                send_sem=pair_sem.at[0],
                recv_sem=pair_sem.at[1],
                device_id=sibling,
                device_id_type=MESH,
            )
            pair.start()
        for lane in range(lanes):
            now[lane].wait_recv()
            if step < devices - 1:
                hops.append(now[lane])
                now[lane] = hop(lane, step)
    hops += now
    for copy in hops:
        copy.wait_send()
    pair.wait()


def spread(stored, target, names, diag):
    nrow = lax.axis_size("row")
    devices = 2 * nrow
    half, cores, width, _ = stored.shape
    parcel = (devices, target.shape[0], target.shape[2] // devices, target.shape[1])
    lanes = 6 if half % 6 == 0 else 2
    return pl.pallas_call(
        functools.partial(spread_kernel, nrow),
        out_shape=(
            jax.ShapeDtypeStruct((devices, half, width, width), stored.dtype),
            jax.ShapeDtypeStruct(parcel, jnp.bfloat16),
            jax.ShapeDtypeStruct(parcel, jnp.bfloat16),
            jax.ShapeDtypeStruct((devices,) + names.shape, names.dtype),
            jax.ShapeDtypeStruct((devices,) + diag.shape, diag.dtype),
        ),
        in_specs=[ANY, pl.BlockSpec(memory_space=pltpu.VMEM), ANY, ANY],
        out_specs=[ANY] * 5,
        scratch_shapes=[
            pltpu.VMEM(parcel, jnp.bfloat16),
            pltpu.SemaphoreType.DMA((lanes, devices - 1)),
            pltpu.SemaphoreType.DMA((lanes, devices - 1)),
            pltpu.SemaphoreType.DMA((3, devices - 1)),
            pltpu.SemaphoreType.DMA((3, devices - 1)),
            pltpu.SemaphoreType.DMA((4,)),
            pltpu.SemaphoreType.DMA((2,)),
        ],
        compiler_params=pltpu.CompilerParams(collective_id=0, has_side_effects=True),
    )(stored, target, names, diag)


def home_kernel(nrow, early, first, parcel, scale, late, field, scales, send, recv, own_sem):
    devices = 2 * nrow
    me = lax.axis_index("row") * 2 + lax.axis_index("col")

    def peer(bits):
        other = flipped(me, bits, devices)
        return {"row": other // 2, "col": lax.rem(other, 2)}

    barrier = pltpu.get_barrier_semaphore()
    for offset in range(1, devices):
        pl.semaphore_signal(barrier, inc=1, device_id=peer(offset), device_id_type=MESH)
    pl.semaphore_wait(barrier, devices - 1)
    copies = []
    rest = pl.ds(early, late.shape[1] - early)
    for n in range(3):
        for offset in range(1, devices):
            to = flipped(me, offset, devices)
            if n == 0:
                source, target = scale, scales.at[me]
            elif n == 2:
                source, target = parcel.at[to], field.at[me]
            elif offset < devices // 2:
                source, target = first.at[to], late.at[me]
            else:
                source, target = first.at[to, rest], late.at[me, rest]
            copy = pltpu.make_async_remote_copy(
                src_ref=source,
                dst_ref=target,
                send_sem=send.at[n, offset - 1],
                recv_sem=recv.at[n, offset - 1],
                device_id=peer(offset),
                device_id_type=MESH,
            )
            copy.start()
            copies.append(copy)
    owns = (
        (scale, scales.at[me]),
        (first.at[me], late.at[me]),
        (parcel.at[me], field.at[me]),
    )
    for n, (source, target) in enumerate(owns):
        copy = pltpu.make_async_copy(source, target, own_sem.at[n])
        copy.start()
        copies.append(copy)
    for copy in copies:
        copy.wait()


def send_home(first, parcel, scale, early):
    nrow = lax.axis_size("row")
    devices = parcel.shape[0]
    return pl.pallas_call(
        functools.partial(home_kernel, nrow, early),
        out_shape=(
            jax.ShapeDtypeStruct(parcel.shape, parcel.dtype),
            jax.ShapeDtypeStruct(parcel.shape, parcel.dtype),
            jax.ShapeDtypeStruct((devices,) + scale.shape, scale.dtype),
        ),
        in_specs=[ANY] * 3,
        out_specs=[ANY] * 3,
        scratch_shapes=[
            pltpu.SemaphoreType.DMA((3, devices - 1)),
            pltpu.SemaphoreType.DMA((3, devices - 1)),
            pltpu.SemaphoreType.DMA((3,)),
        ],
        compiler_params=pltpu.CompilerParams(collective_id=1, has_side_effects=True),
    )(first, parcel, scale)


def finish_kernel(last, me_ref, target_ref, diag_ref, early_ref, late_ref, second_ref, scale_ref,
                  answer_ref, residual_ref, first_ref):
    blocks, width, columns = target_ref.shape
    alpha1, alpha2, beta = scale_ref[0:1], scale_ref[1:2], scale_ref[2:3]
    devices = second_ref.shape[0]
    first_ref[...] = late_ref[...]

    @pl.when(pl.program_id(0) < last)
    def _():
        for far in range(devices // 2):
            first_ref[me_ref[0] ^ (devices // 2 + far)] = early_ref[far]

    diags = diag_ref[...].T
    for b in range(blocks):
        target = target_ref[b]
        diag = diags[:, b : b + 1]
        first = first_ref[:, b].reshape(columns, width).T.astype(jnp.float32)
        second = second_ref[:, b].reshape(columns, width).T.astype(jnp.float32)
        lost = target - target.astype(jnp.bfloat16).astype(jnp.float32)
        lost1 = lost - alpha1 * diag * lost
        answer_ref[b] = alpha1 * target + alpha2 * (first + lost1 + beta * target)
        residual_ref[b] = second + lost1 - alpha2 * diag * (lost1 + beta * lost)


def finish(me, target, diag, early, late, second, scales):
    blocks, width, columns = target.shape
    devices, _, own, _ = second.shape
    step = 8
    last = early.shape[1] // step
    whole = pl.BlockSpec((step, width, columns), lambda g: (g, 0, 0))
    part = pl.BlockSpec((devices, step, own, width), lambda g: (0, g, 0, 0))
    return pl.pallas_call(
        functools.partial(finish_kernel, last),
        out_shape=(jax.ShapeDtypeStruct(target.shape, jnp.float32),) * 2,
        grid=(blocks // step,),
        in_specs=[
            pl.BlockSpec(memory_space=pltpu.SMEM),
            whole,
            pl.BlockSpec((step, width), lambda g: (g, 0)),
            pl.BlockSpec(early.shape[:1] + (step, own, width), lambda g: (0, jnp.minimum(g, last - 1), 0, 0)),
            part,
            part,
            pl.BlockSpec(scales.shape, lambda g: (0, 0)),
        ],
        out_specs=(whole, whole),
        scratch_shapes=[pltpu.VMEM((devices, step, own, width), jnp.bfloat16)],
    )(me, target, diag, early, late, second, scales)


def operate_kernel(slots, irow_ref, icol_ref, count_ref, blocks_ref, mine_ref, theirs_ref,
                   image_ref, away_ref, sum_ref):
    tile = pl.program_id(0)
    own = mine_ref.shape[1]

    @pl.when(tile == 0)
    def _():
        image_ref[...] = jnp.zeros_like(image_ref)
        sum_ref[...] = jnp.zeros_like(sum_ref)

    count = count_ref[tile]

    def group(step, carry):
        base = step * UNROLL
        terms = []
        for u in range(UNROLL):
            k = base + u
            i = irow_ref[tile * slots + k]
            j = icol_ref[tile * slots + k]
            block = blocks_ref[0, k]
            at_i = jnp.concatenate([mine_ref[i], theirs_ref[i]], axis=0)
            at_j = jnp.concatenate([mine_ref[j], theirs_ref[j]], axis=0)
            direct = lax.dot_general(
                at_j, block, (((1,), (1,)), ((), ())), preferred_element_type=jnp.float32
            )
            mirrored = lax.dot_general(
                at_i, block, (((1,), (0,)), ((), ())), preferred_element_type=jnp.float32
            )
            terms.append((k < count, i, j, direct, mirrored))
        for used, i, j, direct, mirrored in terms:
            direct = jnp.where(used, direct, 0.0)
            mirrored = jnp.where(used, mirrored, 0.0)
            image_ref[i] += direct[:own]
            sum_ref[i] += direct[own:]
            image_ref[j] += mirrored[:own]
            sum_ref[j] += mirrored[own:]
        return carry

    lax.fori_loop(0, (count + UNROLL - 1) // UNROLL, group, 0)

    @pl.when(tile == pl.num_programs(0) - 1)
    def _():
        away_ref[...] = sum_ref[...].astype(away_ref.dtype)


def operate(blocks, irow, icol, count, mine, theirs):
    tiles, slots, width, _ = blocks.shape
    whole = pl.BlockSpec(mine.shape, lambda t, *_: (0, 0, 0))
    return pl.pallas_call(
        functools.partial(operate_kernel, slots),
        out_shape=(
            jax.ShapeDtypeStruct(mine.shape, jnp.float32),
            jax.ShapeDtypeStruct(mine.shape, jnp.bfloat16),
        ),
        grid_spec=pltpu.PrefetchScalarGridSpec(
            num_scalar_prefetch=3,
            grid=(tiles,),
            in_specs=[
                pl.BlockSpec((1, slots, width, width), lambda t, *_: (t, 0, 0, 0)),
                whole,
                whole,
            ],
            out_specs=(whole, whole),
            scratch_shapes=[pltpu.VMEM(mine.shape, jnp.float32)],
        ),
        compiler_params=pltpu.CompilerParams(vmem_limit_bytes=40 * 2**20),
        cost_estimate=pl.CostEstimate(
            flops=tiles * slots * width**3 * 4, bytes_accessed=60 * 2**20, transcendentals=0
        ),
    )(irow, icol, count, blocks, mine, theirs)


def by_columns(blocks, block_rows, block_cols, counts, diagonal, target):
    grid = ("row", "col")
    nrow, ncol = lax.axis_size("row"), lax.axis_size("col")
    devices = nrow * ncol
    stored = blocks[0, 0]
    slots, width, _ = stored.shape
    quarter = target.shape[0] // width
    own = target.shape[1] // devices
    row_blocks = ncol * quarter
    half = slots // 2
    row, col, core = lax.axis_index("row"), lax.axis_index("col"), lax.axis_index("rhs")

    irow = row * row_blocks + block_rows[0, 0]
    jcol = block_cols[0, 0]
    icol = (jcol // quarter * ncol + col) * quarter + jcol % quarter

    def every_other(index):
        return jnp.where(core == 0, index[0::2], index[1::2])

    used = (counts[0] - core + 1) // 2
    names = jnp.concatenate([every_other(irow), every_other(icol), used])
    names = jnp.pad(names, (0, -names.shape[0] % 1024)).reshape(-1, 128)
    diag_own = diagonal.reshape(quarter, width)
    target_blocks = target.reshape(quarter, width, target.shape[1])

    tiles, field, field_pair, all_names, all_diag = spread(
        stored.reshape(half, 2, width, width), target_blocks, names, diag_own
    )
    all_names = all_names.reshape(devices, -1)
    irows = all_names[:, :half].reshape(-1)
    icols = all_names[:, half : 2 * half].reshape(-1)
    used = all_names[:, 2 * half]
    diag = all_diag.reshape(-1, 1, width)
    swap = [(0, 1), (1, 0)]

    def image_of(direction, low, theirs, beside=()):
        here, away = operate(tiles, irows, icols, used, low, theirs)
        (here, away), beside = lax.optimization_barrier(((here, away), beside))
        away = lax.ppermute(away, "rhs", swap)
        return diag * direction + here + away.astype(jnp.float32), beside

    def inner(a, b):
        return jnp.sum(a * b, axis=(0, 2), keepdims=True)

    me = row * ncol + col

    def parcels(value):
        return value.astype(jnp.bfloat16).reshape(devices, quarter, own, width)

    def far_home(parcel):
        pieces = []
        for bits in range(devices // 2, devices):
            piece = lax.dynamic_index_in_dim(parcel, me ^ bits, 0, keepdims=False)
            pieces.append(lax.ppermute(piece, grid, [(d, d ^ bits) for d in range(devices)]))
        return pieces

    low = field.reshape(-1, own, width)
    start = low.astype(jnp.float32)
    norm0 = inner(start, start)
    image, _ = image_of(start, low, field_pair.reshape(low.shape))
    alpha1 = norm0 / inner(start, image)
    first = start - alpha1 * image
    norm1 = inner(first, first)
    beta = norm1 / norm0
    direction = first + beta * start
    first_parcel = parcels(first)
    early = quarter // 8 * 5
    pieces = far_home(first_parcel[:, :early])
    low = direction.astype(jnp.bfloat16)
    image, pieces = image_of(direction, low, lax.ppermute(low, "rhs", swap), pieces)
    first_early = jnp.stack(pieces)
    alpha2 = norm1 / inner(direction, image)
    second = first - alpha2 * image
    scale = jnp.stack([alpha1, alpha2, beta]).reshape(3, own)
    scale = jnp.pad(scale, ((0, 5), (0, 128 - own)))
    first_late, second_home, scales = send_home(first_parcel, parcels(second), scale, early)
    scales = scales[:, :3, :own]
    scales = scales.transpose(1, 0, 2).reshape(3, devices * own)
    answer, residual = finish(
        me.reshape(1), target_blocks, diag_own, first_early, first_late, second_home, scales
    )
    return (answer.reshape(target.shape), residual.reshape(target.shape))


def one_hot_slots(indices, valid, extent):
    return ((indices[None, :] == jnp.arange(extent)[:, None]) & valid[None, :]).astype(jnp.float32)


def on_device(blocks, block_rows, block_cols, counts, diagonal, target):
    highest = lax.Precision.HIGHEST
    nrow = lax.axis_size("row")
    ncol = lax.axis_size("col")
    tile_bytes = blocks[0, 0].size * blocks.dtype.itemsize
    if (
        nrow * ncol * tile_bytes <= GATHER_BYTES
        and ncol == 2
        and nrow & (nrow - 1) == 0
        and lax.axis_size("rhs") == 2
        and target.shape[1] == 16 * nrow * ncol
        and blocks.shape[2] % (2 * UNROLL) == 0
        and target.shape[0] // blocks.shape[3] % 64 == 0
    ):
        return by_columns(blocks, block_rows, block_cols, counts, diagonal, target)
    stored = blocks[0, 0]
    slots = stored.shape[0]
    width = stored.shape[1]
    local = target.shape[0]
    ncols = target.shape[1]
    quarter = local // width
    row_blocks = ncol * quarter
    col_blocks = nrow * quarter
    valid = jnp.arange(slots) < counts[0, 0]
    rows_hot = one_hot_slots(block_rows[0, 0], valid, row_blocks)
    cols_hot = one_hot_slots(block_cols[0, 0], valid, col_blocks)

    def squares(vector):
        return lax.psum(jnp.sum(vector * vector, axis=0), ("row", "col"))

    solution = jnp.zeros_like(target)
    residual = target
    direction = target
    norm_now = squares(residual)
    for step in range(ITERS):
        operate_field_low = direction.astype(jnp.bfloat16)
        direct_gathered = lax.all_gather(operate_field_low, "row", axis=0, tiled=True).reshape(
            col_blocks, width, ncols
        )
        prod = jnp.einsum(
            "kab,kbc->kac",
            stored,
            direct_gathered[block_cols[0, 0]],
            preferred_element_type=jnp.float32,
        )
        direct_partial_value = jnp.einsum("ik,kac->iac", rows_hot, prod, precision=highest)
        direct = lax.psum_scatter(
            direct_partial_value.reshape(row_blocks * width, ncols).astype(jnp.bfloat16),
            "col",
            scatter_dimension=0,
            tiled=True,
        ).astype(jnp.float32)
        gathered = lax.all_gather(operate_field_low, "col", axis=0, tiled=True).reshape(
            row_blocks, width, ncols
        )
        tprod = jnp.einsum(
            "kba,kbc->kac", stored, gathered[block_rows[0, 0]], preferred_element_type=jnp.float32
        )
        partial_value = jnp.einsum("jk,kac->jac", cols_hot, tprod, precision=highest)
        parcel = partial_value.astype(jnp.bfloat16).reshape(nrow, local, ncols)
        mirrored = jnp.sum(
            lax.all_to_all(parcel, "row", split_axis=0, concat_axis=0, tiled=True).astype(
                jnp.float32
            ),
            axis=0,
        )
        image = diagonal[:, None] * direction + direct + mirrored
        curve = lax.psum(jnp.sum(direction * image, axis=0), ("row", "col"))
        alpha = norm_now / curve
        solution = solution + alpha * direction
        residual = residual - alpha * image
        if step + 1 < ITERS:
            norm_next = squares(residual)
            direction = residual + norm_next / norm_now * direction
            norm_now = norm_next
    return (solution, residual)


def solution(mesh):
    return jax.shard_map(
        on_device,
        mesh=mesh,
        in_specs=(
            P(("parts", "row"), "col", None, None, None),
            P(("parts", "row"), "col", None),
            P(("parts", "row"), "col", None),
            P(("parts", "row"), "col"),
            P(("parts", "row", "col")),
            P(("parts", "row", "col"), "rhs"),
        ),
        out_specs=(P(("parts", "row", "col"), "rhs"), P(("parts", "row", "col"), "rhs")),
        check_vma=False,
    )
```

```python
import functools
import jax
import jax.numpy as jnp
from jax import lax
from jax.experimental import pallas as pl
from jax.experimental.pallas import tpu as pltpu
from jax.sharding import PartitionSpec as P

ITERS = 2
UNROLL = 8
GATHER_BYTES = 32 * 2**20
MESH = pl.DeviceIdType.MESH
ANY = pl.BlockSpec(memory_space=pl.ANY)


def flipped(index, bits, devices):
    total, unit = index, 1
    while unit < devices:
        if bits & unit:
            total = total + unit * (1 - 2 * lax.rem(index // unit, 2))
        unit *= 2
    return total


def spread_kernel(
    nrow, stored, target, names, diag,
    tiles, field, theirs, all_names, all_diag,
    parcel, ring_send, ring_recv, send, recv, own_sem, pair_sem,
):
    devices = 2 * nrow
    row, col, core = lax.axis_index("row"), lax.axis_index("col"), lax.axis_index("rhs")
    me = row * 2 + col
    place = jnp.where(col == 0, row, devices - 1 - row)

    def device_at(place):
        place = lax.rem(place + devices, devices)
        back = place >= nrow
        return jnp.where(back, devices - 1 - place, place), jnp.where(back, 1, 0)

    def peer(offset):
        other = lax.rem(me + offset, devices)
        return {"row": other // 2, "col": lax.rem(other, 2)}

    barrier = pltpu.get_barrier_semaphore()
    for offset in range(1, devices):
        pl.semaphore_signal(barrier, inc=1, device_id=peer(offset), device_id_type=MESH)
    sibling = {"rhs": 1 - core}
    pl.semaphore_signal(barrier, inc=1, device_id=sibling, device_id_type=MESH)
    pl.semaphore_wait(barrier, devices)

    half = tiles.shape[1]
    lanes = ring_send.shape[0]
    piece = half // lanes
    hops = []

    def hop(lane, step):
        way = lane % 2
        r, c = device_at(place + (1 if way == 0 else -1))
        if step == 0:
            source = stored.at[pl.ds(lane * piece, piece), core]
            origin = me
        else:
            orow, ocol = device_at(place + (-step if way == 0 else step))
            origin = orow * 2 + ocol
            source = tiles.at[origin, pl.ds(lane * piece, piece)]
        copy = pltpu.make_async_remote_copy(
            src_ref=source,
            dst_ref=tiles.at[origin, pl.ds(lane * piece, piece)],
            send_sem=ring_send.at[lane, step],
            recv_sem=ring_recv.at[lane, step],
            device_id={"row": r, "col": c},
            device_id_type=MESH,
        )
        copy.start()
        return copy

    now = [hop(lane, 0) for lane in range(lanes)]

    def pack(b, carry):
        low = target[b].astype(jnp.bfloat16).T
        parcel[:, b] = low.reshape(devices, parcel.shape[2], parcel.shape[3])
        return carry

    lax.fori_loop(0, target.shape[0], pack, 0)
    straight = []
    pairs = ((names, all_names, False), (diag, all_diag, False), (parcel, field, True))
    for n, (source, whole, apart) in enumerate(pairs):
        for offset in range(1, devices):
            copy = pltpu.make_async_remote_copy(
                src_ref=source.at[lax.rem(me + offset, devices)] if apart else source,
                dst_ref=whole.at[me],
                send_sem=send.at[n, offset - 1],
                recv_sem=recv.at[n, offset - 1],
                device_id=peer(offset),
                device_id_type=MESH,
            )
            copy.start()
            straight.append(copy)
    local = []
    owns = (
        (stored.at[:, core], tiles.at[me]),
        (names, all_names.at[me]),
        (diag, all_diag.at[me]),
        (parcel.at[me], field.at[me]),
    )
    for n, (source, whole) in enumerate(owns):
        copy = pltpu.make_async_copy(source, whole, own_sem.at[n])
        copy.start()
        local.append(copy)
    for step in range(1, devices):
        if step == devices - 1:
            for copy in straight:
                copy.wait()
            for copy in local:
                copy.wait()
            pair = pltpu.make_async_remote_copy(
                src_ref=field,
                dst_ref=theirs,
                send_sem=pair_sem.at[0],
                recv_sem=pair_sem.at[1],
                device_id=sibling,
                device_id_type=MESH,
            )
            pair.start()
        for lane in range(lanes):
            now[lane].wait_recv()
            if step < devices - 1:
                hops.append(now[lane])
                now[lane] = hop(lane, step)
    hops += now
    for copy in hops:
        copy.wait_send()
    pair.wait()


def spread(stored, target, names, diag):
    nrow = lax.axis_size("row")
    devices = 2 * nrow
    half, cores, width, _ = stored.shape
    parcel = (devices, target.shape[0], target.shape[2] // devices, target.shape[1])
    lanes = 12 if half % 12 == 0 else 2
    return pl.pallas_call(
        functools.partial(spread_kernel, nrow),
        out_shape=(
            jax.ShapeDtypeStruct((devices, half, width, width), stored.dtype),
            jax.ShapeDtypeStruct(parcel, jnp.bfloat16),
            jax.ShapeDtypeStruct(parcel, jnp.bfloat16),
            jax.ShapeDtypeStruct((devices,) + names.shape, names.dtype),
            jax.ShapeDtypeStruct((devices,) + diag.shape, diag.dtype),
        ),
        in_specs=[ANY, pl.BlockSpec(memory_space=pltpu.VMEM), ANY, ANY],
        out_specs=[ANY] * 5,
        scratch_shapes=[
            pltpu.VMEM(parcel, jnp.bfloat16),
            pltpu.SemaphoreType.DMA((lanes, devices - 1)),
            pltpu.SemaphoreType.DMA((lanes, devices - 1)),
            pltpu.SemaphoreType.DMA((3, devices - 1)),
            pltpu.SemaphoreType.DMA((3, devices - 1)),
            pltpu.SemaphoreType.DMA((4,)),
            pltpu.SemaphoreType.DMA((2,)),
        ],
        compiler_params=pltpu.CompilerParams(collective_id=0, has_side_effects=True),
    )(stored, target, names, diag)


def home_kernel(nrow, early, first, parcel, scale, late, field, scales, send, recv, own_sem):
    devices = 2 * nrow
    me = lax.axis_index("row") * 2 + lax.axis_index("col")

    def peer(bits):
        other = flipped(me, bits, devices)
        return {"row": other // 2, "col": lax.rem(other, 2)}

    barrier = pltpu.get_barrier_semaphore()
    for offset in range(1, devices):
        pl.semaphore_signal(barrier, inc=1, device_id=peer(offset), device_id_type=MESH)
    pl.semaphore_wait(barrier, devices - 1)
    copies = []
    rest = pl.ds(early, late.shape[1] - early)
    for n in range(3):
        for offset in range(1, devices):
            to = flipped(me, offset, devices)
            if n == 0:
                source, target = scale, scales.at[me]
            elif n == 2:
                source, target = parcel.at[to], field.at[me]
            elif offset < devices // 2:
                source, target = first.at[to], late.at[me]
            else:
                source, target = first.at[to, rest], late.at[me, rest]
            copy = pltpu.make_async_remote_copy(
                src_ref=source,
                dst_ref=target,
                send_sem=send.at[n, offset - 1],
                recv_sem=recv.at[n, offset - 1],
                device_id=peer(offset),
                device_id_type=MESH,
            )
            copy.start()
            copies.append(copy)
    owns = (
        (scale, scales.at[me]),
        (first.at[me], late.at[me]),
        (parcel.at[me], field.at[me]),
    )
    for n, (source, target) in enumerate(owns):
        copy = pltpu.make_async_copy(source, target, own_sem.at[n])
        copy.start()
        copies.append(copy)
    for copy in copies:
        copy.wait()


def send_home(first, parcel, scale, early):
    nrow = lax.axis_size("row")
    devices = parcel.shape[0]
    return pl.pallas_call(
        functools.partial(home_kernel, nrow, early),
        out_shape=(
            jax.ShapeDtypeStruct(parcel.shape, parcel.dtype),
            jax.ShapeDtypeStruct(parcel.shape, parcel.dtype),
            jax.ShapeDtypeStruct((devices,) + scale.shape, scale.dtype),
        ),
        in_specs=[ANY] * 3,
        out_specs=[ANY] * 3,
        scratch_shapes=[
            pltpu.SemaphoreType.DMA((3, devices - 1)),
            pltpu.SemaphoreType.DMA((3, devices - 1)),
            pltpu.SemaphoreType.DMA((3,)),
        ],
        compiler_params=pltpu.CompilerParams(collective_id=1, has_side_effects=True),
    )(first, parcel, scale)


def finish_kernel(last, me_ref, target_ref, diag_ref, early_ref, late_ref, second_ref, scale_ref,
                  answer_ref, residual_ref, first_ref):
    blocks, width, columns = target_ref.shape
    alpha1, alpha2, beta = scale_ref[0:1], scale_ref[1:2], scale_ref[2:3]
    devices = second_ref.shape[0]
    first_ref[...] = late_ref[...]

    @pl.when(pl.program_id(0) < last)
    def _():
        for far in range(devices // 2):
            first_ref[me_ref[0] ^ (devices // 2 + far)] = early_ref[far]

    diags = diag_ref[...].T
    for b in range(blocks):
        target = target_ref[b]
        diag = diags[:, b : b + 1]
        first = first_ref[:, b].reshape(columns, width).T.astype(jnp.float32)
        second = second_ref[:, b].reshape(columns, width).T.astype(jnp.float32)
        lost = target - target.astype(jnp.bfloat16).astype(jnp.float32)
        lost1 = lost - alpha1 * diag * lost
        answer_ref[b] = alpha1 * target + alpha2 * (first + lost1 + beta * target)
        residual_ref[b] = second + lost1 - alpha2 * diag * (lost1 + beta * lost)


def finish(me, target, diag, early, late, second, scales):
    blocks, width, columns = target.shape
    devices, _, own, _ = second.shape
    step = 8
    last = early.shape[1] // step
    whole = pl.BlockSpec((step, width, columns), lambda g: (g, 0, 0))
    part = pl.BlockSpec((devices, step, own, width), lambda g: (0, g, 0, 0))
    return pl.pallas_call(
        functools.partial(finish_kernel, last),
        out_shape=(jax.ShapeDtypeStruct(target.shape, jnp.float32),) * 2,
        grid=(blocks // step,),
        in_specs=[
            pl.BlockSpec(memory_space=pltpu.SMEM),
            whole,
            pl.BlockSpec((step, width), lambda g: (g, 0)),
            pl.BlockSpec(early.shape[:1] + (step, own, width), lambda g: (0, jnp.minimum(g, last - 1), 0, 0)),
            part,
            part,
            pl.BlockSpec(scales.shape, lambda g: (0, 0)),
        ],
        out_specs=(whole, whole),
        scratch_shapes=[pltpu.VMEM((devices, step, own, width), jnp.bfloat16)],
    )(me, target, diag, early, late, second, scales)


def operate_kernel(slots, irow_ref, icol_ref, count_ref, blocks_ref, mine_ref, theirs_ref,
                   image_ref, away_ref, sum_ref):
    tile = pl.program_id(0)
    own = mine_ref.shape[1]

    @pl.when(tile == 0)
    def _():
        image_ref[...] = jnp.zeros_like(image_ref)
        sum_ref[...] = jnp.zeros_like(sum_ref)

    count = count_ref[tile]

    def group(step, carry):
        base = step * UNROLL
        terms = []
        for u in range(UNROLL):
            k = base + u
            i = irow_ref[tile * slots + k]
            j = icol_ref[tile * slots + k]
            block = blocks_ref[0, k]
            at_i = jnp.concatenate([mine_ref[i], theirs_ref[i]], axis=0)
            at_j = jnp.concatenate([mine_ref[j], theirs_ref[j]], axis=0)
            direct = lax.dot_general(
                at_j, block, (((1,), (1,)), ((), ())), preferred_element_type=jnp.float32
            )
            mirrored = lax.dot_general(
                at_i, block, (((1,), (0,)), ((), ())), preferred_element_type=jnp.float32
            )
            terms.append((k < count, i, j, direct, mirrored))
        for used, i, j, direct, mirrored in terms:
            direct = jnp.where(used, direct, 0.0)
            mirrored = jnp.where(used, mirrored, 0.0)
            image_ref[i] += direct[:own]
            sum_ref[i] += direct[own:]
            image_ref[j] += mirrored[:own]
            sum_ref[j] += mirrored[own:]
        return carry

    lax.fori_loop(0, (count + UNROLL - 1) // UNROLL, group, 0)

    @pl.when(tile == pl.num_programs(0) - 1)
    def _():
        away_ref[...] = sum_ref[...].astype(away_ref.dtype)


def operate(blocks, irow, icol, count, mine, theirs):
    tiles, slots, width, _ = blocks.shape
    whole = pl.BlockSpec(mine.shape, lambda t, *_: (0, 0, 0))
    return pl.pallas_call(
        functools.partial(operate_kernel, slots),
        out_shape=(
            jax.ShapeDtypeStruct(mine.shape, jnp.float32),
            jax.ShapeDtypeStruct(mine.shape, jnp.bfloat16),
        ),
        grid_spec=pltpu.PrefetchScalarGridSpec(
            num_scalar_prefetch=3,
            grid=(tiles,),
            in_specs=[
                pl.BlockSpec((1, slots, width, width), lambda t, *_: (t, 0, 0, 0)),
                whole,
                whole,
            ],
            out_specs=(whole, whole),
            scratch_shapes=[pltpu.VMEM(mine.shape, jnp.float32)],
        ),
        compiler_params=pltpu.CompilerParams(vmem_limit_bytes=40 * 2**20),
        cost_estimate=pl.CostEstimate(
            flops=tiles * slots * width**3 * 4, bytes_accessed=60 * 2**20, transcendentals=0
        ),
    )(irow, icol, count, blocks, mine, theirs)


def by_columns(blocks, block_rows, block_cols, counts, diagonal, target):
    grid = ("row", "col")
    nrow, ncol = lax.axis_size("row"), lax.axis_size("col")
    devices = nrow * ncol
    stored = blocks[0, 0]
    slots, width, _ = stored.shape
    quarter = target.shape[0] // width
    own = target.shape[1] // devices
    row_blocks = ncol * quarter
    half = slots // 2
    row, col, core = lax.axis_index("row"), lax.axis_index("col"), lax.axis_index("rhs")

    irow = row * row_blocks + block_rows[0, 0]
    jcol = block_cols[0, 0]
    icol = (jcol // quarter * ncol + col) * quarter + jcol % quarter

    def every_other(index):
        return jnp.where(core == 0, index[0::2], index[1::2])

    used = (counts[0] - core + 1) // 2
    names = jnp.concatenate([every_other(irow), every_other(icol), used])
    names = jnp.pad(names, (0, -names.shape[0] % 1024)).reshape(-1, 128)
    diag_own = diagonal.reshape(quarter, width)
    target_blocks = target.reshape(quarter, width, target.shape[1])

    tiles, field, field_pair, all_names, all_diag = spread(
        stored.reshape(half, 2, width, width), target_blocks, names, diag_own
    )
    all_names = all_names.reshape(devices, -1)
    irows = all_names[:, :half].reshape(-1)
    icols = all_names[:, half : 2 * half].reshape(-1)
    used = all_names[:, 2 * half]
    diag = all_diag.reshape(-1, 1, width)
    swap = [(0, 1), (1, 0)]

    def image_of(direction, low, theirs, beside=()):
        here, away = operate(tiles, irows, icols, used, low, theirs)
        (here, away), beside = lax.optimization_barrier(((here, away), beside))
        away = lax.ppermute(away, "rhs", swap)
        return diag * direction + here + away.astype(jnp.float32), beside

    def inner(a, b):
        return jnp.sum(a * b, axis=(0, 2), keepdims=True)

    me = row * ncol + col

    def parcels(value):
        return value.astype(jnp.bfloat16).reshape(devices, quarter, own, width)

    def far_home(parcel):
        pieces = []
        for bits in range(devices // 2, devices):
            piece = lax.dynamic_index_in_dim(parcel, me ^ bits, 0, keepdims=False)
            pieces.append(lax.ppermute(piece, grid, [(d, d ^ bits) for d in range(devices)]))
        return pieces

    low = field.reshape(-1, own, width)
    start = low.astype(jnp.float32)
    norm0 = inner(start, start)
    image, _ = image_of(start, low, field_pair.reshape(low.shape))
    alpha1 = norm0 / inner(start, image)
    first = start - alpha1 * image
    norm1 = inner(first, first)
    beta = norm1 / norm0
    direction = first + beta * start
    first_parcel = parcels(first)
    early = quarter // 8 * 5
    pieces = far_home(first_parcel[:, :early])
    low = direction.astype(jnp.bfloat16)
    image, pieces = image_of(direction, low, lax.ppermute(low, "rhs", swap), pieces)
    first_early = jnp.stack(pieces)
    alpha2 = norm1 / inner(direction, image)
    second = first - alpha2 * image
    scale = jnp.stack([alpha1, alpha2, beta]).reshape(3, own)
    scale = jnp.pad(scale, ((0, 5), (0, 128 - own)))
    first_late, second_home, scales = send_home(first_parcel, parcels(second), scale, early)
    scales = scales[:, :3, :own]
    scales = scales.transpose(1, 0, 2).reshape(3, devices * own)
    answer, residual = finish(
        me.reshape(1), target_blocks, diag_own, first_early, first_late, second_home, scales
    )
    return (answer.reshape(target.shape), residual.reshape(target.shape))


def one_hot_slots(indices, valid, extent):
    return ((indices[None, :] == jnp.arange(extent)[:, None]) & valid[None, :]).astype(jnp.float32)


def on_device(blocks, block_rows, block_cols, counts, diagonal, target):
    highest = lax.Precision.HIGHEST
    nrow = lax.axis_size("row")
    ncol = lax.axis_size("col")
    tile_bytes = blocks[0, 0].size * blocks.dtype.itemsize
    if (
        nrow * ncol * tile_bytes <= GATHER_BYTES
        and ncol == 2
        and nrow & (nrow - 1) == 0
        and lax.axis_size("rhs") == 2
        and target.shape[1] == 16 * nrow * ncol
        and blocks.shape[2] % (2 * UNROLL) == 0
        and target.shape[0] // blocks.shape[3] % 64 == 0
    ):
        return by_columns(blocks, block_rows, block_cols, counts, diagonal, target)
    stored = blocks[0, 0]
    slots = stored.shape[0]
    width = stored.shape[1]
    local = target.shape[0]
    ncols = target.shape[1]
    quarter = local // width
    row_blocks = ncol * quarter
    col_blocks = nrow * quarter
    valid = jnp.arange(slots) < counts[0, 0]
    rows_hot = one_hot_slots(block_rows[0, 0], valid, row_blocks)
    cols_hot = one_hot_slots(block_cols[0, 0], valid, col_blocks)

    def squares(vector):
        return lax.psum(jnp.sum(vector * vector, axis=0), ("row", "col"))

    solution = jnp.zeros_like(target)
    residual = target
    direction = target
    norm_now = squares(residual)
    for step in range(ITERS):
        operate_field_low = direction.astype(jnp.bfloat16)
        direct_gathered = lax.all_gather(operate_field_low, "row", axis=0, tiled=True).reshape(
            col_blocks, width, ncols
        )
        prod = jnp.einsum(
            "kab,kbc->kac",
            stored,
            direct_gathered[block_cols[0, 0]],
            preferred_element_type=jnp.float32,
        )
        direct_partial_value = jnp.einsum("ik,kac->iac", rows_hot, prod, precision=highest)
        direct = lax.psum_scatter(
            direct_partial_value.reshape(row_blocks * width, ncols).astype(jnp.bfloat16),
            "col",
            scatter_dimension=0,
            tiled=True,
        ).astype(jnp.float32)
        gathered = lax.all_gather(operate_field_low, "col", axis=0, tiled=True).reshape(
            row_blocks, width, ncols
        )
        tprod = jnp.einsum(
            "kba,kbc->kac", stored, gathered[block_rows[0, 0]], preferred_element_type=jnp.float32
        )
        partial_value = jnp.einsum("jk,kac->jac", cols_hot, tprod, precision=highest)
        parcel = partial_value.astype(jnp.bfloat16).reshape(nrow, local, ncols)
        mirrored = jnp.sum(
            lax.all_to_all(parcel, "row", split_axis=0, concat_axis=0, tiled=True).astype(
                jnp.float32
            ),
            axis=0,
        )
        image = diagonal[:, None] * direction + direct + mirrored
        curve = lax.psum(jnp.sum(direction * image, axis=0), ("row", "col"))
        alpha = norm_now / curve
        solution = solution + alpha * direction
        residual = residual - alpha * image
        if step + 1 < ITERS:
            norm_next = squares(residual)
            direction = residual + norm_next / norm_now * direction
            norm_now = norm_next
    return (solution, residual)


def solution(mesh):
    return jax.shard_map(
        on_device,
        mesh=mesh,
        in_specs=(
            P(("parts", "row"), "col", None, None, None),
            P(("parts", "row"), "col", None),
            P(("parts", "row"), "col", None),
            P(("parts", "row"), "col"),
            P(("parts", "row", "col")),
            P(("parts", "row", "col"), "rhs"),
        ),
        out_specs=(P(("parts", "row", "col"), "rhs"), P(("parts", "row", "col"), "rhs")),
        check_vma=False,
    )
```

```python
import functools
import jax
import jax.numpy as jnp
from jax import lax
from jax.experimental import pallas as pl
from jax.experimental.pallas import tpu as pltpu
from jax.sharding import PartitionSpec as P

ITERS = 2
UNROLL = 4
GATHER_BYTES = 32 * 2**20
MESH = pl.DeviceIdType.MESH
ANY = pl.BlockSpec(memory_space=pl.ANY)


def flipped(index, bits, devices):
    total, unit = index, 1
    while unit < devices:
        if bits & unit:
            total = total + unit * (1 - 2 * lax.rem(index // unit, 2))
        unit *= 2
    return total


def spread_kernel(
    nrow, stored, target, names, diag,
    tiles, field, theirs, all_names, all_diag,
    parcel, ring_send, ring_recv, send, recv, own_sem, pair_sem,
):
    devices = 2 * nrow
    row, col, core = lax.axis_index("row"), lax.axis_index("col"), lax.axis_index("rhs")
    me = row * 2 + col
    place = jnp.where(col == 0, row, devices - 1 - row)

    def device_at(place):
        place = lax.rem(place + devices, devices)
        back = place >= nrow
        return jnp.where(back, devices - 1 - place, place), jnp.where(back, 1, 0)

    def peer(offset):
        other = lax.rem(me + offset, devices)
        return {"row": other // 2, "col": lax.rem(other, 2)}

    barrier = pltpu.get_barrier_semaphore()
    for offset in range(1, devices):
        pl.semaphore_signal(barrier, inc=1, device_id=peer(offset), device_id_type=MESH)
    sibling = {"rhs": 1 - core}
    pl.semaphore_signal(barrier, inc=1, device_id=sibling, device_id_type=MESH)
    pl.semaphore_wait(barrier, devices)

    half = tiles.shape[1]
    lanes = ring_send.shape[0]
    piece = half // lanes
    hops = []

    def hop(lane, step):
        way = lane % 2
        r, c = device_at(place + (1 if way == 0 else -1))
        if step == 0:
            source = stored.at[pl.ds(lane * piece, piece), core]
            origin = me
        else:
            orow, ocol = device_at(place + (-step if way == 0 else step))
            origin = orow * 2 + ocol
            source = tiles.at[origin, pl.ds(lane * piece, piece)]
        copy = pltpu.make_async_remote_copy(
            src_ref=source,
            dst_ref=tiles.at[origin, pl.ds(lane * piece, piece)],
            send_sem=ring_send.at[lane, step],
            recv_sem=ring_recv.at[lane, step],
            device_id={"row": r, "col": c},
            device_id_type=MESH,
        )
        copy.start()
        return copy

    now = [hop(lane, 0) for lane in range(lanes)]

    def pack(b, carry):
        low = target[b].astype(jnp.bfloat16).T
        parcel[:, b] = low.reshape(devices, parcel.shape[2], parcel.shape[3])
        return carry

    lax.fori_loop(0, target.shape[0], pack, 0)
    straight = []
    pairs = ((names, all_names, False), (diag, all_diag, False), (parcel, field, True))
    for n, (source, whole, apart) in enumerate(pairs):
        for offset in range(1, devices):
            copy = pltpu.make_async_remote_copy(
                src_ref=source.at[lax.rem(me + offset, devices)] if apart else source,
                dst_ref=whole.at[me],
                send_sem=send.at[n, offset - 1],
                recv_sem=recv.at[n, offset - 1],
                device_id=peer(offset),
                device_id_type=MESH,
            )
            copy.start()
            straight.append(copy)
    local = []
    owns = (
        (stored.at[:, core], tiles.at[me]),
        (names, all_names.at[me]),
        (diag, all_diag.at[me]),
        (parcel.at[me], field.at[me]),
    )
    for n, (source, whole) in enumerate(owns):
        copy = pltpu.make_async_copy(source, whole, own_sem.at[n])
        copy.start()
        local.append(copy)
    for step in range(1, devices):
        if step == devices - 1:
            for copy in straight:
                copy.wait()
            for copy in local:
                copy.wait()
            pair = pltpu.make_async_remote_copy(
                src_ref=field,
                dst_ref=theirs,
                send_sem=pair_sem.at[0],
                recv_sem=pair_sem.at[1],
                device_id=sibling,
                device_id_type=MESH,
            )
            pair.start()
        for lane in range(lanes):
            now[lane].wait_recv()
            if step < devices - 1:
                hops.append(now[lane])
                now[lane] = hop(lane, step)
    hops += now
    for copy in hops:
        copy.wait_send()
    pair.wait()


def spread(stored, target, names, diag):
    nrow = lax.axis_size("row")
    devices = 2 * nrow
    half, cores, width, _ = stored.shape
    parcel = (devices, target.shape[0], target.shape[2] // devices, target.shape[1])
    lanes = 12 if half % 12 == 0 else 2
    return pl.pallas_call(
        functools.partial(spread_kernel, nrow),
        out_shape=(
            jax.ShapeDtypeStruct((devices, half, width, width), stored.dtype),
            jax.ShapeDtypeStruct(parcel, jnp.bfloat16),
            jax.ShapeDtypeStruct(parcel, jnp.bfloat16),
            jax.ShapeDtypeStruct((devices,) + names.shape, names.dtype),
            jax.ShapeDtypeStruct((devices,) + diag.shape, diag.dtype),
        ),
        in_specs=[ANY, pl.BlockSpec(memory_space=pltpu.VMEM), ANY, ANY],
        out_specs=[ANY] * 5,
        scratch_shapes=[
            pltpu.VMEM(parcel, jnp.bfloat16),
            pltpu.SemaphoreType.DMA((lanes, devices - 1)),
            pltpu.SemaphoreType.DMA((lanes, devices - 1)),
            pltpu.SemaphoreType.DMA((3, devices - 1)),
            pltpu.SemaphoreType.DMA((3, devices - 1)),
            pltpu.SemaphoreType.DMA((4,)),
            pltpu.SemaphoreType.DMA((2,)),
        ],
        compiler_params=pltpu.CompilerParams(collective_id=0, has_side_effects=True),
    )(stored, target, names, diag)


def home_kernel(nrow, early, first, parcel, scale, late, field, scales, send, recv, own_sem):
    devices = 2 * nrow
    me = lax.axis_index("row") * 2 + lax.axis_index("col")

    def peer(bits):
        other = flipped(me, bits, devices)
        return {"row": other // 2, "col": lax.rem(other, 2)}

    barrier = pltpu.get_barrier_semaphore()
    for offset in range(1, devices):
        pl.semaphore_signal(barrier, inc=1, device_id=peer(offset), device_id_type=MESH)
    pl.semaphore_wait(barrier, devices - 1)
    copies = []
    rest = pl.ds(early, late.shape[1] - early)
    for n in range(3):
        for offset in range(1, devices):
            to = flipped(me, offset, devices)
            if n == 0:
                source, target = scale, scales.at[me]
            elif n == 2:
                source, target = parcel.at[to], field.at[me]
            elif offset < devices // 2:
                source, target = first.at[to], late.at[me]
            else:
                source, target = first.at[to, rest], late.at[me, rest]
            copy = pltpu.make_async_remote_copy(
                src_ref=source,
                dst_ref=target,
                send_sem=send.at[n, offset - 1],
                recv_sem=recv.at[n, offset - 1],
                device_id=peer(offset),
                device_id_type=MESH,
            )
            copy.start()
            copies.append(copy)
    owns = (
        (scale, scales.at[me]),
        (first.at[me], late.at[me]),
        (parcel.at[me], field.at[me]),
    )
    for n, (source, target) in enumerate(owns):
        copy = pltpu.make_async_copy(source, target, own_sem.at[n])
        copy.start()
        copies.append(copy)
    for copy in copies:
        copy.wait()


def send_home(first, parcel, scale, early):
    nrow = lax.axis_size("row")
    devices = parcel.shape[0]
    return pl.pallas_call(
        functools.partial(home_kernel, nrow, early),
        out_shape=(
            jax.ShapeDtypeStruct(parcel.shape, parcel.dtype),
            jax.ShapeDtypeStruct(parcel.shape, parcel.dtype),
            jax.ShapeDtypeStruct((devices,) + scale.shape, scale.dtype),
        ),
        in_specs=[ANY] * 3,
        out_specs=[ANY] * 3,
        scratch_shapes=[
            pltpu.SemaphoreType.DMA((3, devices - 1)),
            pltpu.SemaphoreType.DMA((3, devices - 1)),
            pltpu.SemaphoreType.DMA((3,)),
        ],
        compiler_params=pltpu.CompilerParams(collective_id=1, has_side_effects=True),
    )(first, parcel, scale)


def finish_kernel(last, me_ref, target_ref, diag_ref, early_ref, late_ref, second_ref, scale_ref,
                  answer_ref, residual_ref, first_ref):
    blocks, width, columns = target_ref.shape
    alpha1, alpha2, beta = scale_ref[0:1], scale_ref[1:2], scale_ref[2:3]
    devices = second_ref.shape[0]
    first_ref[...] = late_ref[...]

    @pl.when(pl.program_id(0) < last)
    def _():
        for far in range(devices // 2):
            first_ref[me_ref[0] ^ (devices // 2 + far)] = early_ref[far]

    diags = diag_ref[...].T
    for b in range(blocks):
        target = target_ref[b]
        diag = diags[:, b : b + 1]
        first = first_ref[:, b].reshape(columns, width).T.astype(jnp.float32)
        second = second_ref[:, b].reshape(columns, width).T.astype(jnp.float32)
        lost = target - target.astype(jnp.bfloat16).astype(jnp.float32)
        lost1 = lost - alpha1 * diag * lost
        answer_ref[b] = alpha1 * target + alpha2 * (first + lost1 + beta * target)
        residual_ref[b] = second + lost1 - alpha2 * diag * (lost1 + beta * lost)


def finish(me, target, diag, early, late, second, scales):
    blocks, width, columns = target.shape
    devices, _, own, _ = second.shape
    step = 8
    last = early.shape[1] // step
    whole = pl.BlockSpec((step, width, columns), lambda g: (g, 0, 0))
    part = pl.BlockSpec((devices, step, own, width), lambda g: (0, g, 0, 0))
    return pl.pallas_call(
        functools.partial(finish_kernel, last),
        out_shape=(jax.ShapeDtypeStruct(target.shape, jnp.float32),) * 2,
        grid=(blocks // step,),
        in_specs=[
            pl.BlockSpec(memory_space=pltpu.SMEM),
            whole,
            pl.BlockSpec((step, width), lambda g: (g, 0)),
            pl.BlockSpec(early.shape[:1] + (step, own, width), lambda g: (0, jnp.minimum(g, last - 1), 0, 0)),
            part,
            part,
            pl.BlockSpec(scales.shape, lambda g: (0, 0)),
        ],
        out_specs=(whole, whole),
        scratch_shapes=[pltpu.VMEM((devices, step, own, width), jnp.bfloat16)],
    )(me, target, diag, early, late, second, scales)


def operate_kernel(slots, irow_ref, icol_ref, count_ref, blocks_ref, mine_ref, theirs_ref,
                   image_ref, away_ref, sum_ref):
    tile = pl.program_id(0)
    own = mine_ref.shape[1]

    @pl.when(tile == 0)
    def _():
        image_ref[...] = jnp.zeros_like(image_ref)
        sum_ref[...] = jnp.zeros_like(sum_ref)

    count = count_ref[tile]

    def group(step, carry):
        base = step * UNROLL
        terms = []
        for u in range(UNROLL):
            k = base + u
            i = irow_ref[tile * slots + k]
            j = icol_ref[tile * slots + k]
            block = blocks_ref[0, k]
            at_i = jnp.concatenate([mine_ref[i], theirs_ref[i]], axis=0)
            at_j = jnp.concatenate([mine_ref[j], theirs_ref[j]], axis=0)
            direct = lax.dot_general(
                at_j, block, (((1,), (1,)), ((), ())), preferred_element_type=jnp.float32
            )
            mirrored = lax.dot_general(
                at_i, block, (((1,), (0,)), ((), ())), preferred_element_type=jnp.float32
            )
            terms.append((k < count, i, j, direct, mirrored))
        for used, i, j, direct, mirrored in terms:
            direct = jnp.where(used, direct, 0.0)
            mirrored = jnp.where(used, mirrored, 0.0)
            image_ref[i] += direct[:own]
            sum_ref[i] += direct[own:]
            image_ref[j] += mirrored[:own]
            sum_ref[j] += mirrored[own:]
        return carry

    lax.fori_loop(0, (count + UNROLL - 1) // UNROLL, group, 0)

    @pl.when(tile == pl.num_programs(0) - 1)
    def _():
        away_ref[...] = sum_ref[...].astype(away_ref.dtype)


def operate(blocks, irow, icol, count, mine, theirs):
    tiles, slots, width, _ = blocks.shape
    whole = pl.BlockSpec(mine.shape, lambda t, *_: (0, 0, 0))
    return pl.pallas_call(
        functools.partial(operate_kernel, slots),
        out_shape=(
            jax.ShapeDtypeStruct(mine.shape, jnp.float32),
            jax.ShapeDtypeStruct(mine.shape, jnp.bfloat16),
        ),
        grid_spec=pltpu.PrefetchScalarGridSpec(
            num_scalar_prefetch=3,
            grid=(tiles,),
            in_specs=[
                pl.BlockSpec((1, slots, width, width), lambda t, *_: (t, 0, 0, 0)),
                whole,
                whole,
            ],
            out_specs=(whole, whole),
            scratch_shapes=[pltpu.VMEM(mine.shape, jnp.float32)],
        ),
        compiler_params=pltpu.CompilerParams(vmem_limit_bytes=40 * 2**20),
        cost_estimate=pl.CostEstimate(
            flops=tiles * slots * width**3 * 4, bytes_accessed=60 * 2**20, transcendentals=0
        ),
    )(irow, icol, count, blocks, mine, theirs)


def by_columns(blocks, block_rows, block_cols, counts, diagonal, target):
    grid = ("row", "col")
    nrow, ncol = lax.axis_size("row"), lax.axis_size("col")
    devices = nrow * ncol
    stored = blocks[0, 0]
    slots, width, _ = stored.shape
    quarter = target.shape[0] // width
    own = target.shape[1] // devices
    row_blocks = ncol * quarter
    half = slots // 2
    row, col, core = lax.axis_index("row"), lax.axis_index("col"), lax.axis_index("rhs")

    irow = row * row_blocks + block_rows[0, 0]
    jcol = block_cols[0, 0]
    icol = (jcol // quarter * ncol + col) * quarter + jcol % quarter

    def every_other(index):
        return jnp.where(core == 0, index[0::2], index[1::2])

    used = (counts[0] - core + 1) // 2
    names = jnp.concatenate([every_other(irow), every_other(icol), used])
    names = jnp.pad(names, (0, -names.shape[0] % 1024)).reshape(-1, 128)
    diag_own = diagonal.reshape(quarter, width)
    target_blocks = target.reshape(quarter, width, target.shape[1])

    tiles, field, field_pair, all_names, all_diag = spread(
        stored.reshape(half, 2, width, width), target_blocks, names, diag_own
    )
    all_names = all_names.reshape(devices, -1)
    irows = all_names[:, :half].reshape(-1)
    icols = all_names[:, half : 2 * half].reshape(-1)
    used = all_names[:, 2 * half]
    diag = all_diag.reshape(-1, 1, width)
    swap = [(0, 1), (1, 0)]

    def image_of(direction, low, theirs, beside=()):
        here, away = operate(tiles, irows, icols, used, low, theirs)
        (here, away), beside = lax.optimization_barrier(((here, away), beside))
        away = lax.ppermute(away, "rhs", swap)
        return diag * direction + here + away.astype(jnp.float32), beside

    def inner(a, b):
        return jnp.sum(a * b, axis=(0, 2), keepdims=True)

    me = row * ncol + col

    def parcels(value):
        return value.astype(jnp.bfloat16).reshape(devices, quarter, own, width)

    def far_home(parcel):
        pieces = []
        for bits in range(devices // 2, devices):
            piece = lax.dynamic_index_in_dim(parcel, me ^ bits, 0, keepdims=False)
            pieces.append(lax.ppermute(piece, grid, [(d, d ^ bits) for d in range(devices)]))
        return pieces

    low = field.reshape(-1, own, width)
    start = low.astype(jnp.float32)
    norm0 = inner(start, start)
    image, _ = image_of(start, low, field_pair.reshape(low.shape))
    alpha1 = norm0 / inner(start, image)
    first = start - alpha1 * image
    norm1 = inner(first, first)
    beta = norm1 / norm0
    direction = first + beta * start
    first_parcel = parcels(first)
    early = quarter // 8 * 5
    pieces = far_home(first_parcel[:, :early])
    low = direction.astype(jnp.bfloat16)
    image, pieces = image_of(direction, low, lax.ppermute(low, "rhs", swap), pieces)
    first_early = jnp.stack(pieces)
    alpha2 = norm1 / inner(direction, image)
    second = first - alpha2 * image
    scale = jnp.stack([alpha1, alpha2, beta]).reshape(3, own)
    scale = jnp.pad(scale, ((0, 5), (0, 128 - own)))
    first_late, second_home, scales = send_home(first_parcel, parcels(second), scale, early)
    scales = scales[:, :3, :own]
    scales = scales.transpose(1, 0, 2).reshape(3, devices * own)
    answer, residual = finish(
        me.reshape(1), target_blocks, diag_own, first_early, first_late, second_home, scales
    )
    return (answer.reshape(target.shape), residual.reshape(target.shape))


def one_hot_slots(indices, valid, extent):
    return ((indices[None, :] == jnp.arange(extent)[:, None]) & valid[None, :]).astype(jnp.float32)


def on_device(blocks, block_rows, block_cols, counts, diagonal, target):
    highest = lax.Precision.HIGHEST
    nrow = lax.axis_size("row")
    ncol = lax.axis_size("col")
    tile_bytes = blocks[0, 0].size * blocks.dtype.itemsize
    if (
        nrow * ncol * tile_bytes <= GATHER_BYTES
        and ncol == 2
        and nrow & (nrow - 1) == 0
        and lax.axis_size("rhs") == 2
        and target.shape[1] == 16 * nrow * ncol
        and blocks.shape[2] % (2 * UNROLL) == 0
        and target.shape[0] // blocks.shape[3] % 64 == 0
    ):
        return by_columns(blocks, block_rows, block_cols, counts, diagonal, target)
    stored = blocks[0, 0]
    slots = stored.shape[0]
    width = stored.shape[1]
    local = target.shape[0]
    ncols = target.shape[1]
    quarter = local // width
    row_blocks = ncol * quarter
    col_blocks = nrow * quarter
    valid = jnp.arange(slots) < counts[0, 0]
    rows_hot = one_hot_slots(block_rows[0, 0], valid, row_blocks)
    cols_hot = one_hot_slots(block_cols[0, 0], valid, col_blocks)

    def squares(vector):
        return lax.psum(jnp.sum(vector * vector, axis=0), ("row", "col"))

    solution = jnp.zeros_like(target)
    residual = target
    direction = target
    norm_now = squares(residual)
    for step in range(ITERS):
        operate_field_low = direction.astype(jnp.bfloat16)
        direct_gathered = lax.all_gather(operate_field_low, "row", axis=0, tiled=True).reshape(
            col_blocks, width, ncols
        )
        prod = jnp.einsum(
            "kab,kbc->kac",
            stored,
            direct_gathered[block_cols[0, 0]],
            preferred_element_type=jnp.float32,
        )
        direct_partial_value = jnp.einsum("ik,kac->iac", rows_hot, prod, precision=highest)
        direct = lax.psum_scatter(
            direct_partial_value.reshape(row_blocks * width, ncols).astype(jnp.bfloat16),
            "col",
            scatter_dimension=0,
            tiled=True,
        ).astype(jnp.float32)
        gathered = lax.all_gather(operate_field_low, "col", axis=0, tiled=True).reshape(
            row_blocks, width, ncols
        )
        tprod = jnp.einsum(
            "kba,kbc->kac", stored, gathered[block_rows[0, 0]], preferred_element_type=jnp.float32
        )
        partial_value = jnp.einsum("jk,kac->jac", cols_hot, tprod, precision=highest)
        parcel = partial_value.astype(jnp.bfloat16).reshape(nrow, local, ncols)
        mirrored = jnp.sum(
            lax.all_to_all(parcel, "row", split_axis=0, concat_axis=0, tiled=True).astype(
                jnp.float32
            ),
            axis=0,
        )
        image = diagonal[:, None] * direction + direct + mirrored
        curve = lax.psum(jnp.sum(direction * image, axis=0), ("row", "col"))
        alpha = norm_now / curve
        solution = solution + alpha * direction
        residual = residual - alpha * image
        if step + 1 < ITERS:
            norm_next = squares(residual)
            direction = residual + norm_next / norm_now * direction
            norm_now = norm_next
    return (solution, residual)


def solution(mesh):
    return jax.shard_map(
        on_device,
        mesh=mesh,
        in_specs=(
            P(("parts", "row"), "col", None, None, None),
            P(("parts", "row"), "col", None),
            P(("parts", "row"), "col", None),
            P(("parts", "row"), "col"),
            P(("parts", "row", "col")),
            P(("parts", "row", "col"), "rhs"),
        ),
        out_specs=(P(("parts", "row", "col"), "rhs"), P(("parts", "row", "col"), "rhs")),
        check_vma=False,
    )
```
